32 devices in a mesh: groups: 2 (over y), shard: 4 (over z), sub: 2 (over x), chan: 2 (over core).
Axes of the slice: x: 2, y: 2, z: 4, core: 2. Of those that a mesh axis runs over, the one named last changes fastest.
Arguments:
- field: bfloat16 [32, 8, 96, 128], P(('groups', 'shard'), 'sub', 'chan'), parts along dimension 0, may hold values from -6 to 6
- cotangent: bfloat16 [32, 8, 96, 128], P(('groups', 'shard'), 'sub', 'chan'), parts along dimension 0, may hold values from -6 to 6
- space_weight: bfloat16 [3, 3, 96, 96], replicated, may hold values from -0.21875 to 0.21875
- time_weight: bfloat16 [9, 96], P(None, 'chan'), may hold values from -2 to 2
Outputs:
- output: bfloat16 [32, 8, 96, 128], P(('groups', 'shard'), 'sub', 'chan'), parts along dimension 0
- field_grad: bfloat16 [32, 8, 96, 128], P(('groups', 'shard'), 'sub', 'chan'), parts along dimension 0
- space_grad: float32 [6, 3, 96, 96], P('groups', None, 'chan'), parts along dimension 0
- time_grad: float32 [18, 96], P('groups', 'chan'), parts along dimension 0
The draws below stay inside these ranges and needn't reach their ends.
There are 2 independent parts, one for each index of `groups`. The reference program is written for one: setup_inputs(seed, part) draws one part's arguments, and reference() takes and returns one part's arrays. A program takes and returns all parts, laid end to end along the dimension named above; an argument that names none is the same for every part. Nothing has to cross between parts.
All inputs are finite; a program needn't handle non-finite values.
Results may differ from the reference program's by a relative error of at most 0.0048.
Values may be sent and summed in bfloat16 or wider, within the bound.
A program may use at most 64 MiB of HBM per device.

```python
import jax
import jax.numpy as jnp
from jax import lax

C = 96
W = 128
F = 16
H = 8


def block_levels(rng, shape, split, low, top_value):
    def one(position, blocks):
        draws = jax.random.uniform(jax.random.fold_in(jax.random.fold_in(rng, 6), position), (blocks,), jnp.float32, low / len(split), top_value / len(split))
        return jnp.repeat(jnp.exp(draws), shape[position] // blocks).reshape((-1,) + (1,) * (len(shape) - position - 1))

    gain = one(*split[0])
    for cut in split[1:]:
        gain = gain * one(*cut)
    return gain


def centred(rng, extent, spread, most, pieces=(), held_as=jnp.bfloat16):
    factor_of = block_levels(rng, extent, pieces, -0.22, 0.18) if pieces else 1.0
    result = jax.random.normal(rng, extent, jnp.float32) * spread * factor_of
    return jnp.minimum(jnp.maximum(result, -most), most).astype(held_as)


def setup_inputs(seed: int = 0, part: int = 0) -> dict:
    seeds = jax.random.split(jax.random.key(seed), 5)
    own_keys = jax.random.split(jax.random.fold_in(seeds[4], part), 5)
    return {
        "field": centred(own_keys[0], (F, H, C, W), 1.0, 6.0, ((0, 4), (1, 2), (2, 2))),
        "cotangent": centred(own_keys[1], (F, H, C, W), 1.0, 6.0, ((0, 4), (1, 2), (2, 2))),
        "space_weight": centred(seeds[2], (3, 3, C, C), (9 * C) ** -0.5, 0.21875),
        "time_weight": centred(seeds[3], (9, C), 9 ** -0.5, 2.0, ((1, 2),)),
    }


def gelu_tanh(values):
    return jax.nn.gelu(values, approximate=True)

def pad_frame(frame):
    return jnp.pad(frame, ((1, 1), (0, 0), (1, 1))).astype(jnp.float32)

def space_forward(field, weight):
    rows, cells = (field.shape[1], field.shape[3])

    def one(frame):
        padded = pad_frame(frame)
        total = jnp.zeros((rows, weight.shape[2], cells), jnp.float32)
        for i in range(3):
            for j in range(3):
                total = total + jnp.einsum('oc,rcw->row', weight[i, j].astype(jnp.float32), padded[i:i + rows, :, j:j + cells])
        return total
    return lax.map(one, field)

def space_back(grads, weight):
    rows, cells = (grads.shape[1], grads.shape[3])

    def one(frame):
        padded = pad_frame(frame)
        total = jnp.zeros((rows, weight.shape[3], cells), jnp.float32)
        for i in range(3):
            for j in range(3):
                total = total + jnp.einsum('oc,row->rcw', weight[i, j].astype(jnp.float32), padded[2 - i:2 - i + rows, :, 2 - j:2 - j + cells])
        return total
    return lax.map(one, grads)

def space_weight_grad(field, grads):
    rows, cells, width = (field.shape[1], field.shape[3], field.shape[2])

    def step(carry, pair):
        frame, grad = pair
        padded = pad_frame(frame)
        grad = grad.astype(jnp.float32)
        parts = []
        for i in range(3):
            inner = []
            for j in range(3):
                inner.append(jnp.einsum('row,rcw->oc', grad, padded[i:i + rows, :, j:j + cells]))
            parts.append(jnp.stack(inner))
        return (carry + jnp.stack(parts), None)
    start = jnp.zeros((3, 3, width, width), jnp.float32)
    total, _ = lax.scan(step, start, (field, grads))
    return total

def pad_time(values):
    return jnp.pad(values, ((4, 4), (0, 0), (0, 0), (0, 0)))

def reference(field, cotangent, space_weight, time_weight):
    frames = field.shape[0]
    hidden = space_forward(field, space_weight)
    act, pull = jax.vjp(gelu_tanh, hidden)
    acts = act.astype(jnp.bfloat16)
    taps = time_weight.astype(jnp.float32)
    acts_pad = pad_time(acts)
    mixed = jnp.zeros(field.shape, jnp.float32)
    for k in range(9):
        mixed = mixed + taps[k][:, None] * acts_pad[k:k + frames].astype(jnp.float32)
    mixed = mixed.astype(jnp.bfloat16)
    output = (field.astype(jnp.float32) + mixed.astype(jnp.float32)).astype(jnp.bfloat16)
    grad_pad = pad_time(cotangent)
    back_time = jnp.zeros(field.shape, jnp.float32)
    for k in range(9):
        back_time = back_time + taps[k][:, None] * grad_pad[8 - k:8 - k + frames].astype(jnp.float32)
    back_time = back_time.astype(jnp.bfloat16)
    back_hidden = pull(back_time.astype(jnp.float32))[0].astype(jnp.bfloat16)
    field_grad = (cotangent.astype(jnp.float32) + space_back(back_hidden, space_weight)).astype(jnp.bfloat16)
    scale = float(field.shape[0] * field.shape[1] * field.shape[3]) ** (-0.5)
    space_grad = space_weight_grad(field, back_hidden) * scale
    cot32 = cotangent.astype(jnp.float32)
    time_parts = []
    for k in range(9):
        time_parts.append(lax.optimization_barrier(jnp.sum(cot32 * acts_pad[k:k + frames].astype(jnp.float32), axis=(0, 1, 3))))
    time_grad = jnp.stack(time_parts) * scale
    return (output, field_grad, space_grad, time_grad)
```

```python
import functools

import jax
import jax.numpy as jnp
from jax import lax
from jax.experimental import pallas as pl
from jax.experimental.pallas import tpu as pltpu
from jax.sharding import PartitionSpec as P

F32 = jnp.float32
BF16 = jnp.bfloat16
WIRE = jnp.float32
ROOT = 0.7978845608028654
CUBE = 0.044715
MESH = pl.DeviceIdType.MESH


def block(sizes, field, cot, sw, tw, out, fg, sg, tg,
          xf, bf, ct, ac, gp, wf, wt, wb, tb, rb, rv, rs, fin,
          chan_s, chan_r, halo_s, halo_r, time_s, time_r, red_s, red_r):
    nh, ns, nc, scale = sizes
    frames, rows, own, cells = field.shape
    full = own * nc
    pad = tw.shape[0] // 2
    ntap = tw.shape[0]
    n = nh * ns
    chunk = rv.shape[1]
    s, b, c = lax.axis_index("shard"), lax.axis_index("sub"), lax.axis_index("chan")
    me = s * ns + b
    has_up, has_down = b > 0, b < ns - 1
    has_prev, has_next = s > 0, s < nh - 1
    up, down = lax.rem(b + ns - 1, ns), lax.rem(b + 1, ns)
    prev, nxt = lax.rem(s + nh - 1, nh), lax.rem(s + 1, nh)

    def peer(d):
        other = lax.rem(me + d, n)
        return other, {"shard": other // ns, "sub": lax.rem(other, ns)}

    barrier = pltpu.get_barrier_semaphore()

    def hello(device):
        pl.semaphore_signal(barrier, inc=1, device_id=device, device_id_type=MESH)

    for p in range(1, nc):
        chan = lax.rem(c + p, nc)
        hello({"chan": chan})

        @pl.when(has_up)
        def _():
            hello({"sub": up, "chan": chan})

        @pl.when(has_down)
        def _():
            hello({"sub": down, "chan": chan})

    def hello_peer(d, carry):
        hello(peer(d)[1])
        return carry

    lax.fori_loop(1, n, hello_peer, 0)

    def place(f, carry):
        for r in range(rows):
            xf[c, f, r + 1] = field[f, r]
            ct[f + pad, r] = cot[f, r]
        return carry

    lax.fori_loop(0, frames, place, 0)

    @pl.when(jnp.logical_not(has_up))
    def _():
        for q in range(nc):
            for f in range(frames):
                xf[q, f, 0] = jnp.zeros((own, cells), BF16)
                bf[q, f, 0] = jnp.zeros((own, cells), BF16)

    @pl.when(jnp.logical_not(has_down))
    def _():
        for q in range(nc):
            for f in range(frames):
                xf[q, f, rows + 1] = jnp.zeros((own, cells), BF16)
                bf[q, f, rows + 1] = jnp.zeros((own, cells), BF16)

    @pl.when(jnp.logical_not(has_prev))
    def _():
        for f in range(pad):
            for r in range(rows):
                ct[f, r] = jnp.zeros((own, cells), BF16)
                ac[f, r] = jnp.zeros((own, cells), BF16)

    @pl.when(jnp.logical_not(has_next))
    def _():
        for f in range(pad):
            for r in range(rows):
                ct[frames + pad + f, r] = jnp.zeros((own, cells), BF16)
                ac[frames + pad + f, r] = jnp.zeros((own, cells), BF16)

    mine = pl.ds(pl.multiple_of(c * own, own), own)
    taps_t = jnp.transpose(tw[...].astype(F32))
    for k in range(ntap):
        tb[k] = jnp.broadcast_to(taps_t[:, k : k + 1], (own, cells))
    for i in range(3):
        for j in range(3):
            wf[i, j * own : (j + 1) * own] = sw[i, j, mine]
            wt[...] = jnp.transpose(sw[i, j].astype(F32)).astype(BF16)
            wb[i, j * own : (j + 1) * own] = wt[mine]

    pl.semaphore_wait(
        barrier,
        n - 1 + (nc - 1) * (1 + has_up.astype(jnp.int32) + has_down.astype(jnp.int32)),
    )

    def remote(src, dst, ss, rr, device):
        return pltpu.make_async_remote_copy(
            src_ref=src, dst_ref=dst, send_sem=ss, recv_sem=rr,
            device_id=device, device_id_type=MESH,
        )

    def chan_copies(t, src, dst):
        return [
            remote(src, dst, chan_s.at[t, p - 1], chan_r.at[t, p - 1], {"chan": lax.rem(c + p, nc)})
            for p in range(1, nc)
        ]

    def up_copies(t, src, dst):
        return [
            remote(src, dst, halo_s.at[t, 0, p], halo_r.at[t, 0, p],
                   {"sub": up, "chan": lax.rem(c + p, nc)})
            for p in range(nc)
        ]

    def down_copies(t, src, dst):
        return [
            remote(src, dst, halo_s.at[t, 1, p], halo_r.at[t, 1, p],
                   {"sub": down, "chan": lax.rem(c + p, nc)})
            for p in range(nc)
        ]

    def run(cond, copies, what):
        @pl.when(cond)
        def _():
            for copy in copies:
                getattr(copy, what)()

    x_chan = chan_copies(0, field, xf.at[c, :, 1 : rows + 1])
    x_up = up_copies(0, field.at[:, 0], xf.at[c, :, rows + 1])
    x_down = down_copies(0, field.at[:, rows - 1], xf.at[c, :, 0])
    for copy in x_chan:
        copy.start()
    run(has_up, x_up, "start")
    run(has_down, x_down, "start")

    def time_copies(t, head, tail, buf):
        to_prev = remote(head, buf.at[frames + pad :], time_s.at[t, 0], time_r.at[t, 0], {"shard": prev})
        to_next = remote(tail, buf.at[:pad], time_s.at[t, 1], time_r.at[t, 1], {"shard": nxt})
        return [to_prev], [to_next]

    c_prev, c_next = time_copies(0, cot.at[:pad], cot.at[frames - pad :], ct)
    run(has_prev, c_prev, "start")
    run(has_next, c_next, "start")

    lane = lax.broadcasted_iota(jnp.int32, (own, cells), 1)

    def from_left(v):
        return jnp.where(lane == 0, 0.0, pltpu.roll(v, 1, 1))

    def from_right(v):
        return jnp.where(lane == cells - 1, 0.0, pltpu.roll(v, cells - 1, 1))

    def row_of(buf, f, r):
        return jnp.concatenate([buf[q, f, r] for q in range(nc)], axis=0)

    def rows_of(buf, f):
        return [row_of(buf, f, r) for r in range(rows + 2)]

    rb[...] = jnp.zeros(rb.shape, F32)

    for copy in x_chan:
        copy.wait_recv()
    run(has_down, x_up, "wait_recv")
    run(has_up, x_down, "wait_recv")

    def forward(f, carry):
        line = rows_of(xf, f)
        total = None
        for i in range(3):
            part = jnp.dot(wf[i], jnp.concatenate(line[i : i + rows], axis=1),
                           preferred_element_type=F32)
            total = part if total is None else total + part
        for r in range(rows):
            seg = total[:, r * cells : (r + 1) * cells]
            h = from_left(seg[:own]) + seg[own : 2 * own] + from_right(seg[2 * own :])
            hh = h * h
            t = jnp.tanh(ROOT * (h + CUBE * (hh * h)))
            half = 0.5 * (1.0 + t)
            ac[f + pad, r] = (h * half).astype(BF16)
            gp[f, r] = half + (0.5 * h) * (1.0 - t * t) * (ROOT * (1.0 + (3.0 * CUBE) * hh))
        return carry

    lax.fori_loop(0, frames, forward, 0)

    a_prev, a_next = time_copies(1, ac.at[pad : 2 * pad], ac.at[frames : frames + pad], ac)
    run(has_prev, a_prev, "start")
    run(has_next, a_next, "start")

    run(has_next, c_prev, "wait_recv")
    run(has_prev, c_next, "wait_recv")

    step = 16 if own % 16 == 0 else own
    ones = jnp.ones((8, cells), F32)

    def back(q):
        part = pl.ds(q * step, step)

        def body(r, sums):
            grads = [ct[g, r, part].astype(F32) for g in range(frames + 2 * pad)]
            sums = list(sums)
            for f in range(frames):
                act = ac[f + pad, r, part].astype(F32)
                total = None
                for k in range(ntap):
                    g = grads[f + 2 * pad - k]
                    term = tb[k, part] * g
                    total = term if total is None else total + term
                    sums[k] = sums[k] + act * g
                bt = total.astype(BF16).astype(F32)
                bf[c, f, r + 1, part] = (bt * gp[f, r, part]).astype(BF16)
            return tuple(sums)

        zero = jnp.zeros((step, cells), F32)
        return lax.fori_loop(0, rows, body, (zero,) * ntap)

    pieces = [back(q) for q in range(own // step)]

    g_chan = chan_copies(1, bf.at[c, :, 1 : rows + 1], bf.at[c, :, 1 : rows + 1])
    g_up = up_copies(1, bf.at[c, :, 1], bf.at[c, :, rows + 1])
    g_down = down_copies(1, bf.at[c, :, rows], bf.at[c, :, 0])
    for copy in g_chan:
        copy.start()
    run(has_up, g_up, "start")
    run(has_down, g_down, "start")

    base = 9 * own
    for k in range(ntap):
        whole = jnp.concatenate([piece[k] for piece in pieces], axis=0)
        line = lax.dot_general(ones, whole, (((1,), (1,)), ((), ())),
                               precision=lax.Precision.HIGHEST, preferred_element_type=F32)
        rb[base + k : base + k + 1, :own] = line[:1]

    def weight(f, carry):
        shifted = [[], [], []]
        for r in range(rows):
            v = bf[c, f, r + 1].astype(F32)
            shifted[0].append(from_right(v).astype(BF16))
            shifted[1].append(v.astype(BF16))
            shifted[2].append(from_left(v).astype(BF16))
        left = jnp.concatenate([jnp.concatenate(x, axis=1) for x in shifted], axis=0)
        line = rows_of(xf, f)
        for i in range(3):
            right = jnp.concatenate(line[i : i + rows], axis=1)
            rb[i * 3 * own : (i + 1) * 3 * own] += lax.dot_general(
                left, right, (((1,), (1,)), ((), ())), preferred_element_type=F32
            )
        return carry

    lax.fori_loop(0, frames, weight, 0)

    def scatter(d):
        other, device = peer(d)
        src = rb.at[pl.ds(pl.multiple_of(other * chunk, 8), chunk)]
        return remote(src, rv.at[d - 1], red_s.at[0, d - 1], red_r.at[0, d - 1], device)

    def gather(d):
        _, device = peer(d)
        dst = fin.at[pl.ds(pl.multiple_of(me * chunk, 8), chunk)]
        return remote(rs, dst, red_s.at[1, d - 1], red_r.at[1, d - 1], device)

    def each(make, what):
        def body(d, carry):
            getattr(make(d), what)()
            return carry

        lax.fori_loop(1, n, body, 0)

    each(scatter, "start")

    for copy in g_chan:
        copy.wait_recv()
    run(has_down, g_up, "wait_recv")
    run(has_up, g_down, "wait_recv")

    def backward(f, carry):
        line = rows_of(bf, f)
        total = None
        for i in range(3):
            part = jnp.dot(wb[i], jnp.concatenate(line[2 - i : 2 - i + rows], axis=1),
                           preferred_element_type=F32)
            total = part if total is None else total + part
        for r in range(rows):
            seg = total[:, r * cells : (r + 1) * cells]
            h = from_right(seg[:own]) + seg[own : 2 * own] + from_left(seg[2 * own :])
            fg[f, r] = (cot[f, r].astype(F32) + h).astype(BF16)
        return carry

    lax.fori_loop(0, frames, backward, 0)

    each(scatter, "wait_recv")

    here = pl.ds(pl.multiple_of(me * chunk, 8), chunk)
    total = lax.fori_loop(0, n - 1, lambda d, acc: acc + rv[d], rb[here]) * scale
    rs[...] = total
    fin[here] = total
    each(gather, "start")

    run(has_next, a_prev, "wait_recv")
    run(has_prev, a_next, "wait_recv")

    for q in range(own // step):
        part = pl.ds(q * step, step)

        def mix(r, carry, part=part):
            acts = [ac[g, r, part].astype(F32) for g in range(frames + 2 * pad)]
            for f in range(frames):
                total = None
                for k in range(ntap):
                    term = tb[k, part] * acts[f + k]
                    total = term if total is None else total + term
                mixed = total.astype(BF16).astype(F32)
                out[f, r, part] = (field[f, r, part].astype(F32) + mixed).astype(BF16)
            return carry

        lax.fori_loop(0, rows, mix, 0)

    each(gather, "wait_recv")
    for i in range(3):
        for j in range(3):
            at = (i * 3 + j) * own
            sg[i, j] = fin[at : at + own]
    tg[...] = fin[base : base + ntap, :own]

    for copy in x_chan + g_chan:
        copy.wait_send()
    run(has_up, x_up + g_up, "wait_send")
    run(has_down, x_down + g_down, "wait_send")
    run(has_prev, c_prev + a_prev, "wait_send")
    run(has_next, c_next + a_next, "wait_send")
    each(scatter, "wait_send")
    each(gather, "wait_send")


def on_device(field, cotangent, space_weight, time_weight):
    frames, rows, own, cells = field.shape
    nh, ns, nc = (lax.axis_size(a) for a in ("shard", "sub", "chan"))
    ntap = time_weight.shape[0]
    pad = ntap // 2
    full = own * nc
    n = nh * ns
    need = 9 * own + ntap
    chunk = -(-need // (8 * n)) * 8
    scale = float(frames * nh * rows * ns * cells) ** (-0.5)
    vmem = pl.BlockSpec(memory_space=pltpu.VMEM)
    dma = pltpu.SemaphoreType.DMA
    return pl.pallas_call(
        functools.partial(block, (nh, ns, nc, scale)),
        out_shape=(
            jax.ShapeDtypeStruct(field.shape, BF16),
            jax.ShapeDtypeStruct(field.shape, BF16),
            jax.ShapeDtypeStruct((3, 3, own, full), F32),
            jax.ShapeDtypeStruct((ntap, own), F32),
        ),
        in_specs=[vmem] * 4,
        out_specs=(vmem,) * 4,
        scratch_shapes=[
            pltpu.VMEM((nc, frames, rows + 2, own, cells), BF16),
            pltpu.VMEM((nc, frames, rows + 2, own, cells), BF16),
            pltpu.VMEM((frames + 2 * pad, rows, own, cells), BF16),
            pltpu.VMEM((frames + 2 * pad, rows, own, cells), BF16),
            pltpu.VMEM((frames, rows, own, cells), F32),
            pltpu.VMEM((3, 3 * own, full), BF16),
            pltpu.VMEM((full, full), BF16),
            pltpu.VMEM((3, 3 * own, full), BF16),
            pltpu.VMEM((ntap, own, cells), F32),
            pltpu.VMEM((n * chunk, full), F32),
            pltpu.VMEM((n - 1, chunk, full), F32),
            pltpu.VMEM((chunk, full), F32),
            pltpu.VMEM((n * chunk, full), F32),
            dma((2, nc - 1)),
            dma((2, nc - 1)),
            dma((2, 2, nc)),
            dma((2, 2, nc)),
            dma((2, 2)),
            dma((2, 2)),
            dma((2, n - 1)),
            dma((2, n - 1)),
        ],
        compiler_params=pltpu.CompilerParams(
            collective_id=0, has_side_effects=True, vmem_limit_bytes=60 * 1024 * 1024
        ),
    )(field, cotangent, space_weight, time_weight)


def solution(mesh):
    placed = (
        P(("groups", "shard"), "sub", "chan", None),
        P(("groups", "shard"), "sub", "chan", None),
        P(),
        P(None, "chan"),
    )
    return jax.shard_map(
        on_device,
        mesh=mesh,
        in_specs=placed,
        out_specs=(
            P(("groups", "shard"), "sub", "chan", None),
            P(("groups", "shard"), "sub", "chan", None),
            P("groups", None, "chan", None),
            P("groups", "chan"),
        ),
        check_vma=False,
    )
```

```python
import functools

import jax
import jax.numpy as jnp
from jax import lax
from jax.experimental import pallas as pl
from jax.experimental.pallas import tpu as pltpu
from jax.sharding import PartitionSpec as P

F32 = jnp.float32
BF16 = jnp.bfloat16
WIRE = jnp.float32
ROOT = 0.7978845608028654
CUBE = 0.044715
MESH = pl.DeviceIdType.MESH


def block(sizes, field, cot, sw, tw, out, fg, sg, tg,
          xf, bf, ct, ac, gp, wf, wt, wb, tb, rb, rv, rs, fin,
          swv, twv, load_s, chan_s, chan_r, halo_s, halo_r, time_s, time_r, red_s, red_r):
    nh, ns, nc, scale = sizes
    frames, rows, own, cells = field.shape
    full = own * nc
    pad = tw.shape[0] // 2
    ntap = tw.shape[0]
    n = nh * ns
    chunk = rv.shape[1]
    s, b, c = lax.axis_index("shard"), lax.axis_index("sub"), lax.axis_index("chan")
    me = s * ns + b
    has_up, has_down = b > 0, b < ns - 1
    has_prev, has_next = s > 0, s < nh - 1
    up, down = lax.rem(b + ns - 1, ns), lax.rem(b + 1, ns)
    prev, nxt = lax.rem(s + nh - 1, nh), lax.rem(s + 1, nh)

    def peer(d):
        other = lax.rem(me + d, n)
        return other, {"shard": other // ns, "sub": lax.rem(other, ns)}

    barrier = pltpu.get_barrier_semaphore()

    def hello(device):
        pl.semaphore_signal(barrier, inc=1, device_id=device, device_id_type=MESH)

    for p in range(1, nc):
        chan = lax.rem(c + p, nc)
        hello({"chan": chan})

        @pl.when(has_up)
        def _():
            hello({"sub": up, "chan": chan})

        @pl.when(has_down)
        def _():
            hello({"sub": down, "chan": chan})

    def hello_peer(d, carry):
        hello(peer(d)[1])
        return carry

    lax.fori_loop(1, n, hello_peer, 0)

    loads = [
        pltpu.make_async_copy(src, dst, load_s.at[at])
        for at, (src, dst) in enumerate((
            (tw, twv),
            (sw, swv),
            (field, xf.at[c, :, 1 : rows + 1]),
            (cot, ct.at[pad : pad + frames]),
        ))
    ]
    for load in loads:
        load.start()

    @pl.when(jnp.logical_not(has_up))
    def _():
        for q in range(nc):
            for f in range(frames):
                xf[q, f, 0] = jnp.zeros((own, cells), BF16)
                bf[q, f, 0] = jnp.zeros((own, cells), BF16)

    @pl.when(jnp.logical_not(has_down))
    def _():
        for q in range(nc):
            for f in range(frames):
                xf[q, f, rows + 1] = jnp.zeros((own, cells), BF16)
                bf[q, f, rows + 1] = jnp.zeros((own, cells), BF16)

    @pl.when(jnp.logical_not(has_prev))
    def _():
        for f in range(pad):
            for r in range(rows):
                ct[f, r] = jnp.zeros((own, cells), BF16)
                ac[f, r] = jnp.zeros((own, cells), BF16)

    @pl.when(jnp.logical_not(has_next))
    def _():
        for f in range(pad):
            for r in range(rows):
                ct[frames + pad + f, r] = jnp.zeros((own, cells), BF16)
                ac[frames + pad + f, r] = jnp.zeros((own, cells), BF16)

    mine = pl.ds(pl.multiple_of(c * own, own), own)

    with jax.named_scope("hello"):
        pl.semaphore_wait(
            barrier,
            n - 1 + (nc - 1) * (1 + has_up.astype(jnp.int32) + has_down.astype(jnp.int32)),
        )

    def remote(src, dst, ss, rr, device):
        return pltpu.make_async_remote_copy(
            src_ref=src, dst_ref=dst, send_sem=ss, recv_sem=rr,
            device_id=device, device_id_type=MESH,
        )

    def chan_copies(t, src, dst):
        return [
            remote(src, dst, chan_s.at[t, p - 1], chan_r.at[t, p - 1], {"chan": lax.rem(c + p, nc)})
            for p in range(1, nc)
        ]

    def up_copies(t, src, dst):
        return [
            remote(src, dst, halo_s.at[t, 0, p], halo_r.at[t, 0, p],
                   {"sub": up, "chan": lax.rem(c + p, nc)})
            for p in range(nc)
        ]

    def down_copies(t, src, dst):
        return [
            remote(src, dst, halo_s.at[t, 1, p], halo_r.at[t, 1, p],
                   {"sub": down, "chan": lax.rem(c + p, nc)})
            for p in range(nc)
        ]

    def run(cond, copies, what):
        @pl.when(cond)
        def _():
            for copy in copies:
                getattr(copy, what)()

    x_chan = chan_copies(0, field, xf.at[c, :, 1 : rows + 1])
    x_up = up_copies(0, field.at[:, 0], xf.at[c, :, rows + 1])
    x_down = down_copies(0, field.at[:, rows - 1], xf.at[c, :, 0])
    for copy in x_chan:
        copy.start()
    run(has_up, x_up, "start")
    run(has_down, x_down, "start")

    def time_copies(t, head, tail, buf):
        to_prev = remote(head, buf.at[frames + pad :], time_s.at[t, 0], time_r.at[t, 0], {"shard": prev})
        to_next = remote(tail, buf.at[:pad], time_s.at[t, 1], time_r.at[t, 1], {"shard": nxt})
        return [to_prev], [to_next]

    c_prev, c_next = time_copies(0, cot.at[:pad], cot.at[frames - pad :], ct)
    run(has_prev, c_prev, "start")
    run(has_next, c_next, "start")

    with jax.named_scope("prep"):
        for load in loads[:2]:
            load.wait()
        taps_t = jnp.transpose(twv[...].astype(F32))
        for k in range(ntap):
            tb[k] = jnp.broadcast_to(taps_t[:, k : k + 1], (own, cells))
        for i in range(3):
            for j in range(3):
                wf[i, j * own : (j + 1) * own] = swv[i, j, mine]
                wt[i, j] = jnp.transpose(swv[i, j].astype(F32)).astype(BF16)
        for i in range(3):
            for j in range(3):
                wb[i, j * own : (j + 1) * own] = wt[i, j, mine]
        rb[...] = jnp.zeros(rb.shape, F32)
        for load in loads[2:]:
            load.wait()

    lane = lax.broadcasted_iota(jnp.int32, (own, cells), 1)

    def from_left(v):
        return jnp.where(lane == 0, 0.0, pltpu.roll(v, 1, 1))

    def from_right(v):
        return jnp.where(lane == cells - 1, 0.0, pltpu.roll(v, cells - 1, 1))

    def row_of(buf, f, r):
        return jnp.concatenate([buf[q, f, r] for q in range(nc)], axis=0)

    def rows_of(buf, f):
        return [row_of(buf, f, r) for r in range(rows + 2)]

    with jax.named_scope("wait_x"):
        for copy in x_chan:
            copy.wait_recv()
        run(has_down, x_up, "wait_recv")
        run(has_up, x_down, "wait_recv")

    def forward(f, carry):
        line = rows_of(xf, f)
        total = None
        for i in range(3):
            part = jnp.dot(wf[i], jnp.concatenate(line[i : i + rows], axis=1),
                           preferred_element_type=F32)
            total = part if total is None else total + part
        for r in range(rows):
            seg = total[:, r * cells : (r + 1) * cells]
            h = from_left(seg[:own]) + seg[own : 2 * own] + from_right(seg[2 * own :])
            hh = h * h
            t = jnp.tanh(ROOT * (h + CUBE * (hh * h)))
            half = 0.5 * (1.0 + t)
            ac[f + pad, r] = (h * half).astype(BF16)
            gp[f, r] = half + (0.5 * h) * (1.0 - t * t) * (ROOT * (1.0 + (3.0 * CUBE) * hh))
        return carry

    with jax.named_scope("fwd"):
        lax.fori_loop(0, frames, forward, 0)

    a_prev, a_next = time_copies(1, ac.at[pad : 2 * pad], ac.at[frames : frames + pad], ac)
    run(has_prev, a_prev, "start")
    run(has_next, a_next, "start")

    with jax.named_scope("wait_c"):
        run(has_next, c_prev, "wait_recv")
        run(has_prev, c_next, "wait_recv")

    step = 16 if own % 16 == 0 else own
    ones = jnp.ones((8, cells), F32)

    def back(q):
        part = pl.ds(q * step, step)

        def body(r, sums):
            grads = [ct[g, r, part].astype(F32) for g in range(frames + 2 * pad)]
            sums = list(sums)
            for f in range(frames):
                act = ac[f + pad, r, part].astype(F32)
                total = None
                for k in range(ntap):
                    g = grads[f + 2 * pad - k]
                    term = tb[k, part] * g
                    total = term if total is None else total + term
                    sums[k] = sums[k] + act * g
                bt = total.astype(BF16).astype(F32)
                bf[c, f, r + 1, part] = (bt * gp[f, r, part]).astype(BF16)
            return tuple(sums)

        zero = jnp.zeros((step, cells), F32)
        return lax.fori_loop(0, rows, body, (zero,) * ntap)

    with jax.named_scope("back"):
        pieces = [back(q) for q in range(own // step)]

    g_chan = chan_copies(1, bf.at[c, :, 1 : rows + 1], bf.at[c, :, 1 : rows + 1])
    g_up = up_copies(1, bf.at[c, :, 1], bf.at[c, :, rows + 1])
    g_down = down_copies(1, bf.at[c, :, rows], bf.at[c, :, 0])
    for copy in g_chan:
        copy.start()
    run(has_up, g_up, "start")
    run(has_down, g_down, "start")

    base = 9 * own
    for k in range(ntap):
        whole = jnp.concatenate([piece[k] for piece in pieces], axis=0)
        line = lax.dot_general(ones, whole, (((1,), (1,)), ((), ())),
                               precision=lax.Precision.HIGHEST, preferred_element_type=F32)
        rb[base + k : base + k + 1, :own] = line[:1]

    def weight(f, carry):
        shifted = [[], [], []]
        for r in range(rows):
            v = bf[c, f, r + 1].astype(F32)
            shifted[0].append(from_right(v).astype(BF16))
            shifted[1].append(v.astype(BF16))
            shifted[2].append(from_left(v).astype(BF16))
        left = jnp.concatenate([jnp.concatenate(x, axis=1) for x in shifted], axis=0)
        line = rows_of(xf, f)
        for i in range(3):
            right = jnp.concatenate(line[i : i + rows], axis=1)
            rb[i * 3 * own : (i + 1) * 3 * own] += lax.dot_general(
                left, right, (((1,), (1,)), ((), ())), preferred_element_type=F32
            )
        return carry

    with jax.named_scope("wgt"):
        lax.fori_loop(0, frames, weight, 0)

    def scatter(d):
        other, device = peer(d)
        src = rb.at[pl.ds(pl.multiple_of(other * chunk, 8), chunk)]
        return remote(src, rv.at[d - 1], red_s.at[0, d - 1], red_r.at[0, d - 1], device)

    def gather(d):
        _, device = peer(d)
        dst = fin.at[pl.ds(pl.multiple_of(me * chunk, 8), chunk)]
        return remote(rs, dst, red_s.at[1, d - 1], red_r.at[1, d - 1], device)

    def each(make, what):
        def body(d, carry):
            getattr(make(d), what)()
            return carry

        lax.fori_loop(1, n, body, 0)

    each(scatter, "start")

    with jax.named_scope("wait_g"):
        for copy in g_chan:
            copy.wait_recv()
        run(has_down, g_up, "wait_recv")
        run(has_up, g_down, "wait_recv")

    def backward(f, carry):
        line = rows_of(bf, f)
        total = None
        for i in range(3):
            part = jnp.dot(wb[i], jnp.concatenate(line[2 - i : 2 - i + rows], axis=1),
                           preferred_element_type=F32)
            total = part if total is None else total + part
        for r in range(rows):
            seg = total[:, r * cells : (r + 1) * cells]
            h = from_right(seg[:own]) + seg[own : 2 * own] + from_left(seg[2 * own :])
            fg[f, r] = (ct[f + pad, r].astype(F32) + h).astype(BF16)
        return carry

    with jax.named_scope("bwd"):
        lax.fori_loop(0, frames, backward, 0)

    with jax.named_scope("wait_rs"):
        each(scatter, "wait_recv")

    here = pl.ds(pl.multiple_of(me * chunk, 8), chunk)
    total = lax.fori_loop(0, n - 1, lambda d, acc: acc + rv[d], rb[here]) * scale
    rs[...] = total
    fin[here] = total
    each(gather, "start")

    with jax.named_scope("wait_a"):
        run(has_next, a_prev, "wait_recv")
        run(has_prev, a_next, "wait_recv")

    for q in range(own // step):
        part = pl.ds(q * step, step)

        def mix(r, carry, part=part):
            acts = [ac[g, r, part].astype(F32) for g in range(frames + 2 * pad)]
            for f in range(frames):
                total = None
                for k in range(ntap):
                    term = tb[k, part] * acts[f + k]
                    total = term if total is None else total + term
                mixed = total.astype(BF16).astype(F32)
                out[f, r, part] = (xf[c, f, r + 1, part].astype(F32) + mixed).astype(BF16)
            return carry

        lax.fori_loop(0, rows, mix, 0)

    with jax.named_scope("wait_ag"):
        each(gather, "wait_recv")
    for i in range(3):
        for j in range(3):
            at = (i * 3 + j) * own
            sg[i, j] = fin[at : at + own]
    tg[...] = fin[base : base + ntap, :own]

    for copy in x_chan + g_chan:
        copy.wait_send()
    run(has_up, x_up + g_up, "wait_send")
    run(has_down, x_down + g_down, "wait_send")
    run(has_prev, c_prev + a_prev, "wait_send")
    run(has_next, c_next + a_next, "wait_send")
    each(scatter, "wait_send")
    each(gather, "wait_send")


def ship(*refs):
    sems = refs[8]
    copies = [pltpu.make_async_copy(refs[i], refs[i + 4], sems.at[i]) for i in range(4)]
    for copy in copies:
        copy.start()
    for copy in copies:
        copy.wait()


def on_device(field, cotangent, space_weight, time_weight):
    frames, rows, own, cells = field.shape
    nh, ns, nc = (lax.axis_size(a) for a in ("shard", "sub", "chan"))
    ntap = time_weight.shape[0]
    pad = ntap // 2
    full = own * nc
    n = nh * ns
    need = 9 * own + ntap
    chunk = -(-need // (8 * n)) * 8
    scale = float(frames * nh * rows * ns * cells) ** (-0.5)
    vmem = pl.BlockSpec(memory_space=pltpu.VMEM)
    dma = pltpu.SemaphoreType.DMA
    limit = 20 * 2**20 if rows * frames <= 16 else 56 * 2**20
    hbm = pl.BlockSpec(memory_space=pltpu.HBM)
    shapes = (
        (field.shape, BF16),
        (field.shape, BF16),
        ((3, 3, own, full), F32),
        ((ntap, own), F32),
    )
    held = pl.pallas_call(
        functools.partial(block, (nh, ns, nc, scale)),
        out_shape=tuple(pltpu.VMEM(*x) for x in shapes),
        in_specs=[hbm] * 4,
        out_specs=(vmem,) * 4,
        scratch_shapes=[
            pltpu.VMEM((nc, frames, rows + 2, own, cells), BF16),
            pltpu.VMEM((nc, frames, rows + 2, own, cells), BF16),
            pltpu.VMEM((frames + 2 * pad, rows, own, cells), BF16),
            pltpu.VMEM((frames + 2 * pad, rows, own, cells), BF16),
            pltpu.VMEM((frames, rows, own, cells), F32),
            pltpu.VMEM((3, 3 * own, full), BF16),
            pltpu.VMEM((3, 3, full, full), BF16),
            pltpu.VMEM((3, 3 * own, full), BF16),
            pltpu.VMEM((ntap, own, cells), F32),
            pltpu.VMEM((n * chunk, full), F32),
            pltpu.VMEM((n - 1, chunk, full), F32),
            pltpu.VMEM((chunk, full), F32),
            pltpu.VMEM((n * chunk, full), F32),
            pltpu.VMEM(space_weight.shape, BF16),
            pltpu.VMEM(time_weight.shape, BF16),
            dma((4,)),
            dma((2, nc - 1)),
            dma((2, nc - 1)),
            dma((2, 2, nc)),
            dma((2, 2, nc)),
            dma((2, 2)),
            dma((2, 2)),
            dma((2, n - 1)),
            dma((2, n - 1)),
        ],
        compiler_params=pltpu.CompilerParams(
            collective_id=0, has_side_effects=True, vmem_limit_bytes=limit
        ),
    )(*(pltpu.with_memory_space_constraint(x, pltpu.HBM) for x in (field, cotangent, space_weight, time_weight)))
    return pl.pallas_call(
        ship,
        out_shape=tuple(jax.ShapeDtypeStruct(*x) for x in shapes),
        in_specs=[vmem] * 4,
        out_specs=(hbm,) * 4,
        scratch_shapes=[dma((4,))],
    )(*(pltpu.with_memory_space_constraint(x, pltpu.VMEM) for x in held))


def solution(mesh):
    placed = (
        P(("groups", "shard"), "sub", "chan", None),
        P(("groups", "shard"), "sub", "chan", None),
        P(),
        P(None, "chan"),
    )
    return jax.shard_map(
        on_device,
        mesh=mesh,
        in_specs=placed,
        out_specs=(
            P(("groups", "shard"), "sub", "chan", None),
            P(("groups", "shard"), "sub", "chan", None),
            P("groups", None, "chan", None),
            P("groups", "chan"),
        ),
        check_vma=False,
    )
```

```python
import functools

import jax
import jax.numpy as jnp
from jax import lax
from jax.experimental import pallas as pl
from jax.experimental.pallas import tpu as pltpu
from jax.sharding import PartitionSpec as P

F32 = jnp.float32
BF16 = jnp.bfloat16
ROOT = 0.7978845608028654
CUBE = 0.044715
MESH = pl.DeviceIdType.MESH


def block(sizes, plan, field, cot, sw, tw, out, fg, sg, tg,
          xf, bf, ct, ac, gp, wf, wt, wb, tb, rb, rbb, rv, rs, fin,
          swv, twv, ready, load_s, chan_s, chan_r, halo_s, halo_r, time_s, time_r, red_s, red_r):
    nh, ns, nc, scale = sizes
    frames, rows, own, cells = field.shape
    full = own * nc
    pad = tw.shape[0] // 2
    ntap = tw.shape[0]
    n = nh * ns
    chunk = rv.shape[1]
    s, b, c = lax.axis_index("shard"), lax.axis_index("sub"), lax.axis_index("chan")
    me = s * ns + b
    has_up, has_down = b > 0, b < ns - 1
    has_prev, has_next = s > 0, s < nh - 1
    up, down = lax.rem(b + ns - 1, ns), lax.rem(b + 1, ns)
    prev, nxt = lax.rem(s + nh - 1, nh), lax.rem(s + 1, nh)

    def peer(d):
        other = lax.rem(me + d, n)
        return other, {"shard": other // ns, "sub": lax.rem(other, ns)}

    barrier = pltpu.get_barrier_semaphore()

    def hello(device):
        pl.semaphore_signal(barrier, inc=1, device_id=device, device_id_type=MESH)

    def at(**where):
        return where

    edges = [
        (has_up, at(sub=up)),
        (has_down, at(sub=down)),
        (has_prev, at(shard=prev)),
        (has_next, at(shard=nxt)),
    ]
    sides = sum(has.astype(jnp.int32) for has, _ in edges)
    across = has_up.astype(jnp.int32) + has_down.astype(jnp.int32)

    for p in range(1, nc):
        hello(at(chan=lax.rem(c + p, nc)))
    for has, where in edges:
        @pl.when(has)
        def _(where=where):
            hello(where)
            if "sub" in where:
                for p in range(1, nc):
                    hello(at(chan=lax.rem(c + p, nc), **where))

    rounds = nh + ns - 3

    def tell(t):
        for has, where in edges:
            @pl.when(has)
            def _(where=where):
                pl.semaphore_signal(ready.at[t], inc=1, device_id=where, device_id_type=MESH)

    def heard(t):
        if t < rounds:
            pl.semaphore_wait(ready.at[t], sides)
            if t + 1 < rounds:
                tell(t + 1)

    loads = [
        pltpu.make_async_copy(src, dst, load_s.at[at])
        for at, (src, dst) in enumerate((
            (tw, twv),
            (sw, swv),
            (field, xf.at[c, :, 1 : rows + 1]),
            (cot, ct.at[pad : pad + frames]),
        ))
    ]
    for load in loads:
        load.start()

    @pl.when(jnp.logical_not(has_up))
    def _():
        for q in range(nc):
            for f in range(frames):
                xf[q, f, 0] = jnp.zeros((own, cells), BF16)
                bf[q, f, 0] = jnp.zeros((own, cells), BF16)

    @pl.when(jnp.logical_not(has_down))
    def _():
        for q in range(nc):
            for f in range(frames):
                xf[q, f, rows + 1] = jnp.zeros((own, cells), BF16)
                bf[q, f, rows + 1] = jnp.zeros((own, cells), BF16)

    @pl.when(jnp.logical_not(has_prev))
    def _():
        for f in range(pad):
            for r in range(rows):
                ct[f, r] = jnp.zeros((own, cells), BF16)
                ac[f, r] = jnp.zeros((own, cells), BF16)

    @pl.when(jnp.logical_not(has_next))
    def _():
        for f in range(pad):
            for r in range(rows):
                ct[frames + pad + f, r] = jnp.zeros((own, cells), BF16)
                ac[frames + pad + f, r] = jnp.zeros((own, cells), BF16)

    mine = pl.ds(pl.multiple_of(c * own, own), own)

    with jax.named_scope("hello"):
        pl.semaphore_wait(
            barrier,
            nc - 1 + sides + (nc - 1) * across,
        )
    if rounds > 0:
        tell(0)

    def remote(src, dst, ss, rr, device):
        return pltpu.make_async_remote_copy(
            src_ref=src, dst_ref=dst, send_sem=ss, recv_sem=rr,
            device_id=device, device_id_type=MESH,
        )

    def chan_copies(t, src, dst):
        return [
            remote(src, dst, chan_s.at[t, p - 1], chan_r.at[t, p - 1], {"chan": lax.rem(c + p, nc)})
            for p in range(1, nc)
        ]

    def up_copies(t, src, dst):
        return [
            remote(src, dst, halo_s.at[t, 0, p], halo_r.at[t, 0, p],
                   {"sub": up, "chan": lax.rem(c + p, nc)})
            for p in range(nc)
        ]

    def down_copies(t, src, dst):
        return [
            remote(src, dst, halo_s.at[t, 1, p], halo_r.at[t, 1, p],
                   {"sub": down, "chan": lax.rem(c + p, nc)})
            for p in range(nc)
        ]

    def run(cond, copies, what):
        @pl.when(cond)
        def _():
            for copy in copies:
                getattr(copy, what)()

    x_chan = chan_copies(0, field, xf.at[c, :, 1 : rows + 1])
    x_up = up_copies(0, field.at[:, 0], xf.at[c, :, rows + 1])
    x_down = down_copies(0, field.at[:, rows - 1], xf.at[c, :, 0])
    for copy in x_chan:
        copy.start()
    run(has_up, x_up, "start")
    run(has_down, x_down, "start")

    def time_copies(t, head, tail, buf):
        to_prev = remote(head, buf.at[frames + pad :], time_s.at[t, 0], time_r.at[t, 0], {"shard": prev})
        to_next = remote(tail, buf.at[:pad], time_s.at[t, 1], time_r.at[t, 1], {"shard": nxt})
        return [to_prev], [to_next]

    c_prev, c_next = time_copies(0, cot.at[:pad], cot.at[frames - pad :], ct)
    run(has_prev, c_prev, "start")
    run(has_next, c_next, "start")

    with jax.named_scope("prep"):
        for load in loads[:2]:
            load.wait()
        taps_t = jnp.transpose(twv[...].astype(F32))
        for k in range(ntap):
            tb[k] = jnp.broadcast_to(taps_t[:, k : k + 1], (own, cells))
        for i in range(3):
            for j in range(3):
                wf[i, j * own : (j + 1) * own] = swv[i, j, mine]
                wt[i, j] = jnp.transpose(swv[i, j].astype(F32)).astype(BF16)
        for i in range(3):
            for j in range(3):
                wb[i, j * own : (j + 1) * own] = wt[i, j, mine]
        rb[...] = jnp.zeros(rb.shape, F32)
        for load in loads[2:]:
            load.wait()

    lane = lax.broadcasted_iota(jnp.int32, (own, cells), 1)

    def from_left(v):
        return jnp.where(lane == 0, 0.0, pltpu.roll(v, 1, 1))

    def from_right(v):
        return jnp.where(lane == cells - 1, 0.0, pltpu.roll(v, cells - 1, 1))

    def row_of(buf, f, r):
        return jnp.concatenate([buf[q, f, r] for q in range(nc)], axis=0)

    def rows_of(buf, f):
        return [row_of(buf, f, r) for r in range(rows + 2)]

    with jax.named_scope("wait_x"):
        for copy in x_chan:
            copy.wait_recv()
        run(has_down, x_up, "wait_recv")
        run(has_up, x_down, "wait_recv")

    def forward(f, carry):
        line = rows_of(xf, f)
        total = None
        for i in range(3):
            part = jnp.dot(wf[i], jnp.concatenate(line[i : i + rows], axis=1),
                           preferred_element_type=F32)
            total = part if total is None else total + part
        for r in range(rows):
            seg = total[:, r * cells : (r + 1) * cells]
            h = from_left(seg[:own]) + seg[own : 2 * own] + from_right(seg[2 * own :])
            hh = h * h
            t = jnp.tanh(ROOT * (h + CUBE * (hh * h)))
            half = 0.5 * (1.0 + t)
            ac[f + pad, r] = (h * half).astype(BF16)
            gp[f, r] = half + (0.5 * h) * (1.0 - t * t) * (ROOT * (1.0 + (3.0 * CUBE) * hh))
        return carry

    heard(0)
    with jax.named_scope("fwd"):
        lax.fori_loop(0, frames, forward, 0)

    heard(1)
    with jax.named_scope("wait_c"):
        run(has_next, c_prev, "wait_recv")
        run(has_prev, c_next, "wait_recv")

    half = max(rows // 2, 1)
    a_prev, a_next = [], []
    for t, part in ((1, slice(0, half)), (2, slice(half, rows))):
        to_prev, to_next = time_copies(
            t, ac.at[pad : 2 * pad, part], ac.at[frames : frames + pad, part], ac.at[:, part]
        )
        a_prev += to_prev
        a_next += to_next
    run(has_prev, a_prev[:1], "start")
    run(has_next, a_next[:1], "start")

    step = 16 if own % 16 == 0 else own
    ones = jnp.ones((8, cells), F32)

    def back(q):
        part = pl.ds(q * step, step)

        def body(r, sums):
            grads = [ct[g, r, part].astype(F32) for g in range(frames + 2 * pad)]
            sums = list(sums)
            for f in range(frames):
                act = ac[f + pad, r, part].astype(F32)
                total = None
                for k in range(ntap):
                    g = grads[f + 2 * pad - k]
                    term = tb[k, part] * g
                    total = term if total is None else total + term
                    sums[k] = sums[k] + act * g
                bt = total.astype(BF16).astype(F32)
                bf[c, f, r + 1, part] = (bt * gp[f, r, part]).astype(BF16)
            return tuple(sums)

        zero = jnp.zeros((step, cells), F32)
        return lax.fori_loop(0, rows, body, (zero,) * ntap)

    with jax.named_scope("back"):
        sums = [back(q) for q in range(own // step)]

    g_chan = chan_copies(1, bf.at[c, :, 1 : rows + 1], bf.at[c, :, 1 : rows + 1])
    g_up = up_copies(1, bf.at[c, :, 1], bf.at[c, :, rows + 1])
    g_down = down_copies(1, bf.at[c, :, rows], bf.at[c, :, 0])
    for copy in g_chan:
        copy.start()
    run(has_up, g_up, "start")
    run(has_down, g_down, "start")

    base = 9 * own
    for k in range(ntap):
        whole = jnp.concatenate([piece[k] for piece in sums], axis=0)
        line = lax.dot_general(ones, whole, (((1,), (1,)), ((), ())),
                               precision=lax.Precision.HIGHEST, preferred_element_type=F32)
        rb[base + k : base + k + 1, :own] = line[:1]

    def weight(f, carry):
        shifted = [[], [], []]
        for r in range(rows):
            v = bf[c, f, r + 1].astype(F32)
            shifted[0].append(from_right(v).astype(BF16))
            shifted[1].append(v.astype(BF16))
            shifted[2].append(from_left(v).astype(BF16))
        left = jnp.concatenate([jnp.concatenate(x, axis=1) for x in shifted], axis=0)
        line = rows_of(xf, f)
        for i in range(3):
            right = jnp.concatenate(line[i : i + rows], axis=1)
            rb[i * 3 * own : (i + 1) * 3 * own, :full] += lax.dot_general(
                left, right, (((1,), (1,)), ((), ())), preferred_element_type=F32
            )
        return carry

    with jax.named_scope("wgt"):
        lax.fori_loop(0, frames, weight, 0)

    def scatter(d):
        other, device = peer(d)
        src = rbb.at[pl.ds(pl.multiple_of(other * chunk, 16), chunk)]
        return remote(src, rv.at[d - 1], red_s.at[0, d - 1], red_r.at[0, d - 1], device)

    def gather(d):
        _, device = peer(d)
        dst = fin.at[pl.ds(pl.multiple_of(me * chunk, 16), chunk)]
        return remote(rs, dst, red_s.at[1, d - 1], red_r.at[1, d - 1], device)

    def each(make, what):
        def body(d, carry):
            getattr(make(d), what)()
            return carry

        lax.fori_loop(1, n, body, 0)

    spare, pieces, extra = plan
    packed = rb.shape[0] - extra
    if packed < rbb.shape[0]:
        rbb[packed:] = jnp.zeros((rbb.shape[0] - packed, rbb.shape[1]), BF16)
    if pieces:
        lanes = rb.shape[1]
        place = lax.broadcasted_iota(jnp.int32, (extra, lanes), 1)
        tail = rb[packed:]
        for t in range(pieces):
            mixed = jnp.where(
                place < full,
                rb[t * extra : (t + 1) * extra],
                pltpu.roll(tail, (full - t * spare) % lanes, 1),
            )
            rbb[t * extra : (t + 1) * extra] = mixed.astype(BF16)
    else:
        rbb[:packed] = rb[...].astype(BF16)
    for t in range(2, rounds):
        heard(t)
    each(scatter, "start")
    run(has_prev, a_prev[1:], "start")
    run(has_next, a_next[1:], "start")

    with jax.named_scope("wait_g"):
        for copy in g_chan:
            copy.wait_recv()
        run(has_down, g_up, "wait_recv")
        run(has_up, g_down, "wait_recv")

    def backward(f, carry):
        line = rows_of(bf, f)
        total = None
        for i in range(3):
            part = jnp.dot(wb[i], jnp.concatenate(line[2 - i : 2 - i + rows], axis=1),
                           preferred_element_type=F32)
            total = part if total is None else total + part
        for r in range(rows):
            seg = total[:, r * cells : (r + 1) * cells]
            h = from_right(seg[:own]) + seg[own : 2 * own] + from_left(seg[2 * own :])
            fg[f, r] = (ct[f + pad, r].astype(F32) + h).astype(BF16)
        return carry

    with jax.named_scope("bwd"):
        lax.fori_loop(0, frames, backward, 0)

    with jax.named_scope("wait_rs"):
        each(scatter, "wait_recv")

    here = pl.ds(pl.multiple_of(me * chunk, 16), chunk)
    total = lax.fori_loop(0, n - 1, lambda d, acc: acc + rv[d].astype(F32), rbb[here].astype(F32)) * scale
    rs[...] = total.astype(BF16)
    fin[here] = total.astype(BF16)
    each(gather, "start")

    with jax.named_scope("wait_a"):
        run(has_next, a_prev, "wait_recv")
        run(has_prev, a_next, "wait_recv")

    for q in range(own // step):
        part = pl.ds(q * step, step)

        def mix(r, carry, part=part):
            acts = [ac[g, r, part].astype(F32) for g in range(frames + 2 * pad)]
            for f in range(frames):
                total = None
                for k in range(ntap):
                    term = tb[k, part] * acts[f + k]
                    total = term if total is None else total + term
                mixed = total.astype(BF16).astype(F32)
                out[f, r, part] = (xf[c, f, r + 1, part].astype(F32) + mixed).astype(BF16)
            return carry

        lax.fori_loop(0, rows, mix, 0)

    with jax.named_scope("wait_ag"):
        each(gather, "wait_recv")
    if pieces:
        last = None
        for t in reversed(range(pieces)):
            v = fin[t * extra : (t + 1) * extra].astype(F32)
            rb[t * extra : (t + 1) * extra] = v
            v = pltpu.roll(v, (t * spare - full) % lanes, 1)
            last = v if last is None else jnp.where(place < (t + 1) * spare, v, last)
        rb[packed:] = last
    else:
        rb[...] = fin[:packed].astype(F32)
    for i in range(3):
        for j in range(3):
            top = (i * 3 + j) * own
            sg[i, j] = rb[top : top + own, :full]
    tg[...] = rb[base : base + ntap, :own]

    for copy in x_chan + g_chan:
        copy.wait_send()
    run(has_up, x_up + g_up, "wait_send")
    run(has_down, x_down + g_down, "wait_send")
    run(has_prev, c_prev + a_prev, "wait_send")
    run(has_next, c_next + a_next, "wait_send")
    each(scatter, "wait_send")
    each(gather, "wait_send")


def ship(*refs):
    sems = refs[8]
    copies = [pltpu.make_async_copy(refs[i], refs[i + 4], sems.at[i]) for i in range(4)]
    for copy in copies:
        copy.start()
    for copy in copies:
        copy.wait()


def on_device(field, cotangent, space_weight, time_weight):
    frames, rows, own, cells = field.shape
    nh, ns, nc = (lax.axis_size(a) for a in ("shard", "sub", "chan"))
    ntap = time_weight.shape[0]
    pad = ntap // 2
    full = own * nc
    n = nh * ns
    need = 9 * own + ntap
    lanes = -(-full // 128) * 128
    spare = lanes - full
    if spare and full % spare == 0:
        pieces = full // spare
        extra = -(-need // (16 * (pieces + 1))) * 16
        packed = extra * pieces
    else:
        pieces, extra, packed = 0, 0, -(-need // 16) * 16
    chunk = -(-packed // (16 * n)) * 16
    scale = float(frames * nh * rows * ns * cells) ** (-0.5)
    vmem = pl.BlockSpec(memory_space=pltpu.VMEM)
    dma = pltpu.SemaphoreType.DMA
    limit = 20 * 2**20 if rows * frames <= 16 else 56 * 2**20
    hbm = pl.BlockSpec(memory_space=pltpu.HBM)
    shapes = (
        (field.shape, BF16),
        (field.shape, BF16),
        ((3, 3, own, full), F32),
        ((ntap, own), F32),
    )
    held = pl.pallas_call(
        functools.partial(block, (nh, ns, nc, scale), (spare, pieces, extra)),
        out_shape=tuple(pltpu.VMEM(*x) for x in shapes),
        in_specs=[hbm] * 4,
        out_specs=(vmem,) * 4,
        scratch_shapes=[
            pltpu.VMEM((nc, frames, rows + 2, own, cells), BF16),
            pltpu.VMEM((nc, frames, rows + 2, own, cells), BF16),
            pltpu.VMEM((frames + 2 * pad, rows, own, cells), BF16),
            pltpu.VMEM((frames + 2 * pad, rows, own, cells), BF16),
            pltpu.VMEM((frames, rows, own, cells), F32),
            pltpu.VMEM((3, 3 * own, full), BF16),
            pltpu.VMEM((3, 3, full, full), BF16),
            pltpu.VMEM((3, 3 * own, full), BF16),
            pltpu.VMEM((ntap, own, cells), F32),
            pltpu.VMEM((packed + extra, lanes), F32),
            pltpu.VMEM((n * chunk, lanes), BF16),
            pltpu.VMEM((n - 1, chunk, lanes), BF16),
            pltpu.VMEM((chunk, lanes), BF16),
            pltpu.VMEM((n * chunk, lanes), BF16),
            pltpu.VMEM(space_weight.shape, BF16),
            pltpu.VMEM(time_weight.shape, BF16),
            pltpu.SemaphoreType.REGULAR((max(nh + ns - 3, 1),)),
            dma((4,)),
            dma((2, nc - 1)),
            dma((2, nc - 1)),
            dma((2, 2, nc)),
            dma((2, 2, nc)),
            dma((3, 2)),
            dma((3, 2)),
            dma((2, n - 1)),
            dma((2, n - 1)),
        ],
        compiler_params=pltpu.CompilerParams(
            collective_id=0, has_side_effects=True, vmem_limit_bytes=limit
        ),
    )(*(pltpu.with_memory_space_constraint(x, pltpu.HBM) for x in (field, cotangent, space_weight, time_weight)))
    return pl.pallas_call(
        ship,
        out_shape=tuple(jax.ShapeDtypeStruct(*x) for x in shapes),
        in_specs=[vmem] * 4,
        out_specs=(hbm,) * 4,
        scratch_shapes=[dma((4,))],
    )(*(pltpu.with_memory_space_constraint(x, pltpu.VMEM) for x in held))


def solution(mesh):
    placed = (
        P(("groups", "shard"), "sub", "chan", None),
        P(("groups", "shard"), "sub", "chan", None),
        P(),
        P(None, "chan"),
    )
    return jax.shard_map(
        on_device,
        mesh=mesh,
        in_specs=placed,
        out_specs=(
            P(("groups", "shard"), "sub", "chan", None),
            P(("groups", "shard"), "sub", "chan", None),
            P("groups", None, "chan", None),
            P("groups", "chan"),
        ),
        check_vma=False,
    )
```

```python
import functools

import jax
import jax.numpy as jnp
from jax import lax
from jax.experimental import pallas as pl
from jax.experimental.pallas import tpu as pltpu
from jax.sharding import PartitionSpec as P

F32 = jnp.float32
BF16 = jnp.bfloat16
ROOT = 0.7978845608028654
CUBE = 0.044715
MESH = pl.DeviceIdType.MESH


def block(sizes, plan, field, cot, sw, tw, out, fg, sg, tg,
          xf, bf, ct, ac, gp, wf, wt, wb, tb, rb, rbb, rv, rs, fin,
          swv, twv, ready, load_s, chan_s, chan_r, halo_s, halo_r, time_s, time_r, red_s, red_r):
    nh, ns, nc, scale = sizes
    frames, rows, own, cells = field.shape
    full = own * nc
    pad = tw.shape[0] // 2
    ntap = tw.shape[0]
    n = nh * ns
    chunk = rv.shape[1]
    parts = row_parts(rows)
    s, b, c = lax.axis_index("shard"), lax.axis_index("sub"), lax.axis_index("chan")
    me = s * ns + b
    has_up, has_down = b > 0, b < ns - 1
    has_prev, has_next = s > 0, s < nh - 1
    up, down = lax.rem(b + ns - 1, ns), lax.rem(b + 1, ns)
    prev, nxt = lax.rem(s + nh - 1, nh), lax.rem(s + 1, nh)

    def peer(d):
        other = lax.rem(me + d, n)
        return other, {"shard": other // ns, "sub": lax.rem(other, ns)}

    barrier = pltpu.get_barrier_semaphore()

    def hello(device):
        pl.semaphore_signal(barrier, inc=1, device_id=device, device_id_type=MESH)

    def at(**where):
        return where

    edges = [
        (has_up, at(sub=up)),
        (has_down, at(sub=down)),
        (has_prev, at(shard=prev)),
        (has_next, at(shard=nxt)),
    ]
    sides = sum(has.astype(jnp.int32) for has, _ in edges)
    across = has_up.astype(jnp.int32) + has_down.astype(jnp.int32)

    for p in range(1, nc):
        hello(at(chan=lax.rem(c + p, nc)))
    for has, where in edges:
        @pl.when(has)
        def _(where=where):
            hello(where)
            if "sub" in where:
                for p in range(1, nc):
                    hello(at(chan=lax.rem(c + p, nc), **where))

    rounds = nh + ns - 3

    def tell(t):
        for has, where in edges:
            @pl.when(has)
            def _(where=where):
                pl.semaphore_signal(ready.at[t], inc=1, device_id=where, device_id_type=MESH)

    def heard(t):
        if t < rounds:
            pl.semaphore_wait(ready.at[t], sides)
            if t + 1 < rounds:
                tell(t + 1)

    loads = [
        pltpu.make_async_copy(src, dst, load_s.at[at])
        for at, (src, dst) in enumerate((
            (tw, twv),
            (sw, swv),
            (field, xf.at[c, :, 1 : rows + 1]),
            (cot, ct.at[pad : pad + frames]),
        ))
    ]
    for load in loads:
        load.start()

    @pl.when(jnp.logical_not(has_up))
    def _():
        for q in range(nc):
            for f in range(frames):
                xf[q, f, 0] = jnp.zeros((own, cells), BF16)
                bf[q, f, 0] = jnp.zeros((own, cells), BF16)

    @pl.when(jnp.logical_not(has_down))
    def _():
        for q in range(nc):
            for f in range(frames):
                xf[q, f, rows + 1] = jnp.zeros((own, cells), BF16)
                bf[q, f, rows + 1] = jnp.zeros((own, cells), BF16)

    @pl.when(jnp.logical_not(has_prev))
    def _():
        for f in range(pad):
            for r in range(rows):
                ct[f, r] = jnp.zeros((own, cells), BF16)
                ac[f, r] = jnp.zeros((own, cells), BF16)

    @pl.when(jnp.logical_not(has_next))
    def _():
        for f in range(pad):
            for r in range(rows):
                ct[frames + pad + f, r] = jnp.zeros((own, cells), BF16)
                ac[frames + pad + f, r] = jnp.zeros((own, cells), BF16)

    mine = pl.ds(pl.multiple_of(c * own, own), own)

    with jax.named_scope("hello"):
        pl.semaphore_wait(
            barrier,
            nc - 1 + sides + (nc - 1) * across,
        )
    if rounds > 0:
        tell(0)

    def remote(src, dst, ss, rr, device):
        return pltpu.make_async_remote_copy(
            src_ref=src, dst_ref=dst, send_sem=ss, recv_sem=rr,
            device_id=device, device_id_type=MESH,
        )

    def chan_copies(t, src, dst):
        return [
            remote(src, dst, chan_s.at[t, p - 1], chan_r.at[t, p - 1], {"chan": lax.rem(c + p, nc)})
            for p in range(1, nc)
        ]

    def up_copies(t, src, dst):
        return [
            remote(src, dst, halo_s.at[t, 0, p], halo_r.at[t, 0, p],
                   {"sub": up, "chan": lax.rem(c + p, nc)})
            for p in range(nc)
        ]

    def down_copies(t, src, dst):
        return [
            remote(src, dst, halo_s.at[t, 1, p], halo_r.at[t, 1, p],
                   {"sub": down, "chan": lax.rem(c + p, nc)})
            for p in range(nc)
        ]

    def run(cond, copies, what):
        @pl.when(cond)
        def _():
            for copy in copies:
                getattr(copy, what)()

    x_chan = chan_copies(0, field, xf.at[c, :, 1 : rows + 1])
    x_up = up_copies(0, field.at[:, 0], xf.at[c, :, rows + 1])
    x_down = down_copies(0, field.at[:, rows - 1], xf.at[c, :, 0])
    for copy in x_chan:
        copy.start()
    run(has_up, x_up, "start")
    run(has_down, x_down, "start")

    def time_copies(t, head, tail, buf):
        to_prev = remote(head, buf.at[frames + pad :], time_s.at[t, 0], time_r.at[t, 0], {"shard": prev})
        to_next = remote(tail, buf.at[:pad], time_s.at[t, 1], time_r.at[t, 1], {"shard": nxt})
        return [to_prev], [to_next]

    c_prev, c_next = [], []
    for t, (lo, hi) in enumerate(parts):
        to_prev, to_next = time_copies(
            t, cot.at[:pad, lo:hi], cot.at[frames - pad :, lo:hi], ct.at[:, lo:hi]
        )
        c_prev += to_prev
        c_next += to_next
        run(has_prev, to_prev, "start")
        run(has_next, to_next, "start")

    with jax.named_scope("prep"):
        for load in loads[:2]:
            load.wait()
        taps_t = jnp.transpose(twv[...].astype(F32))
        for k in range(ntap):
            tb[k] = jnp.broadcast_to(taps_t[:, k : k + 1], (own, cells))
        for i in range(3):
            for j in range(3):
                wf[i, j * own : (j + 1) * own] = swv[i, j, mine]
                wt[i, j] = jnp.transpose(swv[i, j].astype(F32)).astype(BF16)
        for i in range(3):
            for j in range(3):
                wb[i, j * own : (j + 1) * own] = wt[i, j, mine]
        rb[...] = jnp.zeros(rb.shape, F32)
        for load in loads[2:]:
            load.wait()

    lane = lax.broadcasted_iota(jnp.int32, (own, cells), 1)

    def from_left(v):
        return jnp.where(lane == 0, 0.0, pltpu.roll(v, 1, 1))

    def from_right(v):
        return jnp.where(lane == cells - 1, 0.0, pltpu.roll(v, cells - 1, 1))

    def row_of(buf, f, r):
        return jnp.concatenate([buf[q, f, r] for q in range(nc)], axis=0)

    def rows_of(buf, f):
        return [row_of(buf, f, r) for r in range(rows + 2)]

    with jax.named_scope("wait_x"):
        for copy in x_chan:
            copy.wait_recv()
        run(has_down, x_up, "wait_recv")
        run(has_up, x_down, "wait_recv")

    def forward(f, carry):
        line = rows_of(xf, f)
        total = None
        for i in range(3):
            part = jnp.dot(wf[i], jnp.concatenate(line[i : i + rows], axis=1),
                           preferred_element_type=F32)
            total = part if total is None else total + part
        for r in range(rows):
            seg = total[:, r * cells : (r + 1) * cells]
            h = from_left(seg[:own]) + seg[own : 2 * own] + from_right(seg[2 * own :])
            hh = h * h
            t = jnp.tanh(ROOT * (h + CUBE * (hh * h)))
            half = 0.5 * (1.0 + t)
            ac[f + pad, r] = (h * half).astype(BF16)
            gp[f, r] = half + (0.5 * h) * (1.0 - t * t) * (ROOT * (1.0 + (3.0 * CUBE) * hh))
        return carry

    heard(0)
    with jax.named_scope("fwd"):
        lax.fori_loop(0, frames, forward, 0, unroll=True)

    heard(1)
    half = max(rows // 2, 1)
    a_prev, a_next = [], []
    for t, part in ((len(parts), slice(0, half)), (len(parts) + 1, slice(half, rows))):
        to_prev, to_next = time_copies(
            t, ac.at[pad : 2 * pad, part], ac.at[frames : frames + pad, part], ac.at[:, part]
        )
        a_prev += to_prev
        a_next += to_next
    step = 16 if own % 16 == 0 else own

    def back(q, lo, hi, begin):
        part = pl.ds(q * step, step)

        def body(r, sums):
            grads = [ct[g, r, part].astype(F32) for g in range(frames + 2 * pad)]
            sums = list(sums)
            for f in range(frames):
                act = ac[f + pad, r, part].astype(F32)
                total = None
                for k in range(ntap):
                    g = grads[f + 2 * pad - k]
                    term = tb[k, part] * g
                    total = term if total is None else total + term
                    sums[k] = sums[k] + act * g
                bt = total.astype(BF16).astype(F32)
                bf[c, f, r + 1, part] = (bt * gp[f, r, part]).astype(BF16)
            return tuple(sums)

        return lax.fori_loop(lo, hi, body, begin)

    def weight(lo, hi):
        shifted = [[], [], []]
        right = [[], [], []]
        for f in range(frames):
            line = [row_of(xf, f, r) for r in range(lo, hi + 2)]
            for r in range(lo, hi):
                v = bf[c, f, r + 1].astype(F32)
                shifted[0].append(from_right(v).astype(BF16))
                shifted[1].append(v.astype(BF16))
                shifted[2].append(from_left(v).astype(BF16))
                for i in range(3):
                    right[i].append(line[r - lo + i])
        left = jnp.concatenate([jnp.concatenate(x, axis=1) for x in shifted], axis=0)
        for i in range(3):
            rb[i * 3 * own : (i + 1) * 3 * own, :full] += lax.dot_general(
                left, jnp.concatenate(right[i], axis=1), (((1,), (1,)), ((), ())),
                preferred_element_type=F32,
            )

    sums = [(jnp.zeros((step, cells), F32),) * ntap] * (own // step)
    g_chan = []
    g_up = up_copies(1, bf.at[c, :, 1], bf.at[c, :, rows + 1])
    g_down = down_copies(1, bf.at[c, :, rows], bf.at[c, :, 0])
    base = 9 * own
    for t, (lo, hi) in enumerate(parts):
        with jax.named_scope("wait_c"):
            run(has_next, c_prev[t : t + 1], "wait_recv")
            run(has_prev, c_next[t : t + 1], "wait_recv")
        final = t == len(parts) - 1
        if final:
            run(has_prev, a_prev[:1], "start")
            run(has_next, a_next[:1], "start")
        with jax.named_scope("back"):
            sums = [back(q, lo, hi, sums[q]) for q in range(own // step)]
        lines = bf.at[c, :, 1 + lo : 1 + hi]
        sent = chan_copies(1 + t, lines, lines)
        g_chan += sent
        for copy in sent:
            copy.start()
        if t == 0:
            run(has_up, g_up, "start")
        if final:
            run(has_down, g_down, "start")
            whole = jnp.concatenate([sums[q][k] for k in range(ntap) for q in range(own // step)], axis=0)
            high = whole.astype(BF16)
            rest = whole - high.astype(F32)
            middle = rest.astype(BF16)
            low = (rest - middle.astype(F32)).astype(BF16)
            line = lax.dot_general(
                jnp.ones((16, 3 * cells), BF16), jnp.concatenate([high, middle, low], axis=1),
                (((1,), (1,)), ((), ())), preferred_element_type=F32,
            )
            for k in range(ntap):
                rb[base + k : base + k + 1, :own] = line[:1, k * own : (k + 1) * own]
        with jax.named_scope("wgt"):
            weight(lo, hi)

    def scatter(d):
        other, device = peer(d)
        src = rbb.at[pl.ds(pl.multiple_of(other * chunk, 16), chunk)]
        return remote(src, rv.at[d - 1], red_s.at[0, d - 1], red_r.at[0, d - 1], device)

    def gather(d):
        _, device = peer(d)
        dst = fin.at[pl.ds(pl.multiple_of(me * chunk, 16), chunk)]
        return remote(rs, dst, red_s.at[1, d - 1], red_r.at[1, d - 1], device)

    def each(make, what):
        def body(d, carry):
            getattr(make(d), what)()
            return carry

        lax.fori_loop(1, n, body, 0)

    spare, pieces, extra = plan
    packed = rb.shape[0] - extra
    if packed < rbb.shape[0]:
        rbb[packed:] = jnp.zeros((rbb.shape[0] - packed, rbb.shape[1]), BF16)
    if pieces:
        lanes = rb.shape[1]
        place = lax.broadcasted_iota(jnp.int32, (extra, lanes), 1)
        tail = rb[packed:]
        for t in range(pieces):
            mixed = jnp.where(
                place < full,
                rb[t * extra : (t + 1) * extra],
                pltpu.roll(tail, (full - t * spare) % lanes, 1),
            )
            rbb[t * extra : (t + 1) * extra] = mixed.astype(BF16)
    else:
        rbb[:packed] = rb[...].astype(BF16)
    for t in range(2, rounds):
        heard(t)
    each(scatter, "start")
    run(has_prev, a_prev[1:], "start")
    run(has_next, a_next[1:], "start")

    with jax.named_scope("wait_g"):
        for copy in g_chan:
            copy.wait_recv()
        run(has_down, g_up, "wait_recv")
        run(has_up, g_down, "wait_recv")

    def backward(f, carry):
        line = rows_of(bf, f)
        total = None
        for i in range(3):
            part = jnp.dot(wb[i], jnp.concatenate(line[2 - i : 2 - i + rows], axis=1),
                           preferred_element_type=F32)
            total = part if total is None else total + part
        for r in range(rows):
            seg = total[:, r * cells : (r + 1) * cells]
            h = from_right(seg[:own]) + seg[own : 2 * own] + from_left(seg[2 * own :])
            fg[f, r] = (ct[f + pad, r].astype(F32) + h).astype(BF16)
        return carry

    with jax.named_scope("bwd"):
        lax.fori_loop(0, frames, backward, 0, unroll=True)

    with jax.named_scope("wait_rs"):
        each(scatter, "wait_recv")

    here = pl.ds(pl.multiple_of(me * chunk, 16), chunk)
    total = lax.fori_loop(0, n - 1, lambda d, acc: acc + rv[d].astype(F32), rbb[here].astype(F32)) * scale
    rs[...] = total.astype(BF16)
    fin[here] = total.astype(BF16)
    each(gather, "start")

    with jax.named_scope("wait_a"):
        run(has_next, a_prev, "wait_recv")
        run(has_prev, a_next, "wait_recv")

    for q in range(own // step):
        part = pl.ds(q * step, step)

        def mix(r, carry, part=part):
            acts = [ac[g, r, part].astype(F32) for g in range(frames + 2 * pad)]
            for f in range(frames):
                total = None
                for k in range(ntap):
                    term = tb[k, part] * acts[f + k]
                    total = term if total is None else total + term
                mixed = total.astype(BF16).astype(F32)
                out[f, r, part] = (xf[c, f, r + 1, part].astype(F32) + mixed).astype(BF16)
            return carry

        lax.fori_loop(0, rows, mix, 0)

    with jax.named_scope("wait_ag"):
        each(gather, "wait_recv")
    if pieces:
        last = None
        for t in reversed(range(pieces)):
            v = fin[t * extra : (t + 1) * extra].astype(F32)
            rb[t * extra : (t + 1) * extra] = v
            v = pltpu.roll(v, (t * spare - full) % lanes, 1)
            last = v if last is None else jnp.where(place < (t + 1) * spare, v, last)
        rb[packed:] = last
    else:
        rb[...] = fin[:packed].astype(F32)
    for i in range(3):
        for j in range(3):
            top = (i * 3 + j) * own
            sg[i, j] = rb[top : top + own, :full]
    tg[...] = rb[base : base + ntap, :own]

    for copy in x_chan + g_chan:
        copy.wait_send()
    run(has_up, x_up + g_up, "wait_send")
    run(has_down, x_down + g_down, "wait_send")
    run(has_prev, c_prev + a_prev, "wait_send")
    run(has_next, c_next + a_next, "wait_send")
    each(scatter, "wait_send")
    each(gather, "wait_send")


def row_parts(rows):
    first = max(rows // 2, 1)
    second = first + max((rows - first) // 2, 0)
    cuts = sorted({0, first, second, rows})
    return list(zip(cuts[:-1], cuts[1:]))


def ship(*refs):
    sems = refs[8]
    copies = [pltpu.make_async_copy(refs[i], refs[i + 4], sems.at[i]) for i in range(4)]
    for copy in copies:
        copy.start()
    for copy in copies:
        copy.wait()


def on_device(field, cotangent, space_weight, time_weight):
    frames, rows, own, cells = field.shape
    nh, ns, nc = (lax.axis_size(a) for a in ("shard", "sub", "chan"))
    ntap = time_weight.shape[0]
    pad = ntap // 2
    full = own * nc
    n = nh * ns
    need = 9 * own + ntap
    lanes = -(-full // 128) * 128
    spare = lanes - full
    if spare and full % spare == 0:
        pieces = full // spare
        extra = -(-need // (16 * (pieces + 1))) * 16
        packed = extra * pieces
    else:
        pieces, extra, packed = 0, 0, -(-need // 16) * 16
    chunk = -(-packed // (16 * n)) * 16
    scale = float(frames * nh * rows * ns * cells) ** (-0.5)
    vmem = pl.BlockSpec(memory_space=pltpu.VMEM)
    dma = pltpu.SemaphoreType.DMA
    count = len(row_parts(rows))
    limit = 20 * 2**20 if rows * frames <= 16 else 56 * 2**20
    hbm = pl.BlockSpec(memory_space=pltpu.HBM)
    shapes = (
        (field.shape, BF16),
        (field.shape, BF16),
        ((3, 3, own, full), F32),
        ((ntap, own), F32),
    )
    held = pl.pallas_call(
        functools.partial(block, (nh, ns, nc, scale), (spare, pieces, extra)),
        out_shape=tuple(pltpu.VMEM(*x) for x in shapes),
        in_specs=[hbm] * 4,
        out_specs=(vmem,) * 4,
        scratch_shapes=[
            pltpu.VMEM((nc, frames, rows + 2, own, cells), BF16),
            pltpu.VMEM((nc, frames, rows + 2, own, cells), BF16),
            pltpu.VMEM((frames + 2 * pad, rows, own, cells), BF16),
            pltpu.VMEM((frames + 2 * pad, rows, own, cells), BF16),
            pltpu.VMEM((frames, rows, own, cells), F32),
            pltpu.VMEM((3, 3 * own, full), BF16),
            pltpu.VMEM((3, 3, full, full), BF16),
            pltpu.VMEM((3, 3 * own, full), BF16),
            pltpu.VMEM((ntap, own, cells), F32),
            pltpu.VMEM((packed + extra, lanes), F32),
            pltpu.VMEM((n * chunk, lanes), BF16),
            pltpu.VMEM((n - 1, chunk, lanes), BF16),
            pltpu.VMEM((chunk, lanes), BF16),
            pltpu.VMEM((n * chunk, lanes), BF16),
            pltpu.VMEM(space_weight.shape, BF16),
            pltpu.VMEM(time_weight.shape, BF16),
            pltpu.SemaphoreType.REGULAR((max(nh + ns - 3, 1),)),
            dma((4,)),
            dma((count + 1, nc - 1)),
            dma((count + 1, nc - 1)),
            dma((2, 2, nc)),
            dma((2, 2, nc)),
            dma((count + 2, 2)),
            dma((count + 2, 2)),
            dma((2, n - 1)),
            dma((2, n - 1)),
        ],
        compiler_params=pltpu.CompilerParams(
            collective_id=0, has_side_effects=True, vmem_limit_bytes=limit
        ),
    )(*(pltpu.with_memory_space_constraint(x, pltpu.HBM) for x in (field, cotangent, space_weight, time_weight)))
    return pl.pallas_call(
        ship,
        out_shape=tuple(jax.ShapeDtypeStruct(*x) for x in shapes),
        in_specs=[vmem] * 4,
        out_specs=(hbm,) * 4,
        scratch_shapes=[dma((4,))],
    )(*(pltpu.with_memory_space_constraint(x, pltpu.VMEM) for x in held))


def solution(mesh):
    placed = (
        P(("groups", "shard"), "sub", "chan", None),
        P(("groups", "shard"), "sub", "chan", None),
        P(),
        P(None, "chan"),
    )
    return jax.shard_map(
        on_device,
        mesh=mesh,
        in_specs=placed,
        out_specs=(
            P(("groups", "shard"), "sub", "chan", None),
            P(("groups", "shard"), "sub", "chan", None),
            P("groups", None, "chan", None),
            P("groups", "chan"),
        ),
        check_vma=False,
    )
```

```python
import functools

import jax
import jax.numpy as jnp
from jax import lax
from jax.experimental import pallas as pl
from jax.experimental.pallas import tpu as pltpu
from jax.sharding import PartitionSpec as P

F32 = jnp.float32
BF16 = jnp.bfloat16
ROOT = 0.7978845608028654
CUBE = 0.044715
MESH = pl.DeviceIdType.MESH


def block(sizes, plan, field, cot, sw, tw, out, fg, sg, tg,
          xf, bf, ct, ac, gp, wf, wt, wb, tb, rb, rbb, rv, rs, fin,
          swv, twv, ready, load_s, chan_s, chan_r, halo_s, halo_r, time_s, time_r, red_s, red_r):
    nh, ns, nc, scale = sizes
    frames, rows, own, cells = field.shape
    full = own * nc
    pad = tw.shape[0] // 2
    ntap = tw.shape[0]
    n = nh * ns
    chunk = rv.shape[1]
    parts = row_parts(rows)
    s, b, c = lax.axis_index("shard"), lax.axis_index("sub"), lax.axis_index("chan")
    me = s * ns + b
    has_up, has_down = b > 0, b < ns - 1
    has_prev, has_next = s > 0, s < nh - 1
    up, down = lax.rem(b + ns - 1, ns), lax.rem(b + 1, ns)
    prev, nxt = lax.rem(s + nh - 1, nh), lax.rem(s + 1, nh)

    def peer(d):
        other = lax.rem(me + d, n)
        return other, {"shard": other // ns, "sub": lax.rem(other, ns)}

    barrier = pltpu.get_barrier_semaphore()

    def hello(device):
        pl.semaphore_signal(barrier, inc=1, device_id=device, device_id_type=MESH)

    def at(**where):
        return where

    edges = [
        (has_up, at(sub=up)),
        (has_down, at(sub=down)),
        (has_prev, at(shard=prev)),
        (has_next, at(shard=nxt)),
    ]
    sides = sum(has.astype(jnp.int32) for has, _ in edges)
    across = has_up.astype(jnp.int32) + has_down.astype(jnp.int32)

    for p in range(1, nc):
        hello(at(chan=lax.rem(c + p, nc)))
    for has, where in edges:
        @pl.when(has)
        def _(where=where):
            hello(where)
            if "sub" in where:
                for p in range(1, nc):
                    hello(at(chan=lax.rem(c + p, nc), **where))

    rounds = nh + ns - 3

    def tell(t):
        for has, where in edges:
            @pl.when(has)
            def _(where=where):
                pl.semaphore_signal(ready.at[t], inc=1, device_id=where, device_id_type=MESH)

    def heard(t):
        if t < rounds:
            pl.semaphore_wait(ready.at[t], sides)
            if t + 1 < rounds:
                tell(t + 1)

    loads = [
        pltpu.make_async_copy(src, dst, load_s.at[at])
        for at, (src, dst) in enumerate((
            (tw, twv),
            (sw, swv),
            (field, xf.at[c, :, 1 : rows + 1]),
            (cot, ct.at[pad : pad + frames]),
        ))
    ]
    for load in loads:
        load.start()

    @pl.when(jnp.logical_not(has_up))
    def _():
        for q in range(nc):
            for f in range(frames):
                xf[q, f, 0] = jnp.zeros((own, cells), BF16)
                bf[q, f, 0] = jnp.zeros((own, cells), BF16)

    @pl.when(jnp.logical_not(has_down))
    def _():
        for q in range(nc):
            for f in range(frames):
                xf[q, f, rows + 1] = jnp.zeros((own, cells), BF16)
                bf[q, f, rows + 1] = jnp.zeros((own, cells), BF16)

    @pl.when(jnp.logical_not(has_prev))
    def _():
        for f in range(pad):
            for r in range(rows):
                ct[f, r] = jnp.zeros((own, cells), BF16)
                ac[f, r] = jnp.zeros((own, cells), BF16)

    @pl.when(jnp.logical_not(has_next))
    def _():
        for f in range(pad):
            for r in range(rows):
                ct[frames + pad + f, r] = jnp.zeros((own, cells), BF16)
                ac[frames + pad + f, r] = jnp.zeros((own, cells), BF16)

    mine = pl.ds(pl.multiple_of(c * own, own), own)

    with jax.named_scope("hello"):
        pl.semaphore_wait(
            barrier,
            nc - 1 + sides + (nc - 1) * across,
        )
    if rounds > 0:
        tell(0)

    def remote(src, dst, ss, rr, device):
        return pltpu.make_async_remote_copy(
            src_ref=src, dst_ref=dst, send_sem=ss, recv_sem=rr,
            device_id=device, device_id_type=MESH,
        )

    def chan_copies(t, src, dst):
        return [
            remote(src, dst, chan_s.at[t, p - 1], chan_r.at[t, p - 1], {"chan": lax.rem(c + p, nc)})
            for p in range(1, nc)
        ]

    def up_copies(t, src, dst):
        return [
            remote(src, dst, halo_s.at[t, 0, p], halo_r.at[t, 0, p],
                   {"sub": up, "chan": lax.rem(c + p, nc)})
            for p in range(nc)
        ]

    def down_copies(t, src, dst):
        return [
            remote(src, dst, halo_s.at[t, 1, p], halo_r.at[t, 1, p],
                   {"sub": down, "chan": lax.rem(c + p, nc)})
            for p in range(nc)
        ]

    def run(cond, copies, what):
        @pl.when(cond)
        def _():
            for copy in copies:
                getattr(copy, what)()

    x_chan = chan_copies(0, field, xf.at[c, :, 1 : rows + 1])
    x_up = up_copies(0, field.at[:, 0], xf.at[c, :, rows + 1])
    x_down = down_copies(0, field.at[:, rows - 1], xf.at[c, :, 0])
    for copy in x_chan:
        copy.start()
    run(has_up, x_up, "start")
    run(has_down, x_down, "start")

    def time_copies(t, head, tail, buf):
        to_prev = remote(head, buf.at[frames + pad :], time_s.at[t, 0], time_r.at[t, 0], {"shard": prev})
        to_next = remote(tail, buf.at[:pad], time_s.at[t, 1], time_r.at[t, 1], {"shard": nxt})
        return [to_prev], [to_next]

    c_prev, c_next = [], []
    for t, (lo, hi) in enumerate(parts):
        to_prev, to_next = time_copies(
            t, cot.at[:pad, lo:hi], cot.at[frames - pad :, lo:hi], ct.at[:, lo:hi]
        )
        c_prev += to_prev
        c_next += to_next
        run(has_prev, to_prev, "start")
        run(has_next, to_next, "start")

    with jax.named_scope("prep"):
        for load in loads[:2]:
            load.wait()
        taps_t = jnp.transpose(twv[...].astype(F32))
        for k in range(ntap):
            tb[k] = jnp.broadcast_to(taps_t[:, k : k + 1], (own, cells))
        for i in range(3):
            for j in range(3):
                wf[i, j * own : (j + 1) * own] = swv[i, j, mine]
                wt[i, j] = jnp.transpose(swv[i, j].astype(F32)).astype(BF16)
        for i in range(3):
            for j in range(3):
                wb[i, j * own : (j + 1) * own] = wt[i, j, mine]
        rb[...] = jnp.zeros(rb.shape, F32)
        for load in loads[2:]:
            load.wait()

    lane = lax.broadcasted_iota(jnp.int32, (own, cells), 1)

    def from_left(v):
        return jnp.where(lane == 0, 0.0, pltpu.roll(v, 1, 1))

    def from_right(v):
        return jnp.where(lane == cells - 1, 0.0, pltpu.roll(v, cells - 1, 1))

    def row_of(buf, f, r):
        return jnp.concatenate([buf[q, f, r] for q in range(nc)], axis=0)

    def rows_of(buf, f):
        return [row_of(buf, f, r) for r in range(rows + 2)]

    with jax.named_scope("wait_x"):
        for copy in x_chan:
            copy.wait_recv()
        run(has_down, x_up, "wait_recv")
        run(has_up, x_down, "wait_recv")

    def forward(f, carry):
        line = rows_of(xf, f)
        total = None
        for i in range(3):
            part = jnp.dot(wf[i], jnp.concatenate(line[i : i + rows], axis=1),
                           preferred_element_type=F32)
            total = part if total is None else total + part
        for r in range(rows):
            seg = total[:, r * cells : (r + 1) * cells]
            h = from_left(seg[:own]) + seg[own : 2 * own] + from_right(seg[2 * own :])
            hh = h * h
            t = jnp.tanh(ROOT * (h + CUBE * (hh * h)))
            half = 0.5 * (1.0 + t)
            ac[f + pad, r] = (h * half).astype(BF16)
            gp[f, r] = half + (0.5 * h) * (1.0 - t * t) * (ROOT * (1.0 + (3.0 * CUBE) * hh))
        return carry

    heard(0)
    with jax.named_scope("fwd"):
        lax.fori_loop(0, frames, forward, 0, unroll=True)

    a_prev, a_next = [], []
    for t, (lo, hi) in enumerate(parts):
        part = slice(lo, hi)
        to_prev, to_next = time_copies(
            len(parts) + t, ac.at[pad : 2 * pad, part], ac.at[frames : frames + pad, part], ac.at[:, part]
        )
        a_prev += to_prev
        a_next += to_next
    run(has_prev, a_prev[:1], "start")
    run(has_next, a_next[:1], "start")
    step = 16 if own % 16 == 0 else own

    def back(q, lo, hi, begin):
        part = pl.ds(q * step, step)

        def body(r, sums):
            grads = [ct[g, r, part].astype(F32) for g in range(frames + 2 * pad)]
            sums = list(sums)
            for f in range(frames):
                act = ac[f + pad, r, part].astype(F32)
                total = None
                for k in range(ntap):
                    g = grads[f + 2 * pad - k]
                    term = tb[k, part] * g
                    total = term if total is None else total + term
                    sums[k] = sums[k] + act * g
                bt = total.astype(BF16).astype(F32)
                bf[c, f, r + 1, part] = (bt * gp[f, r, part]).astype(BF16)
            return tuple(sums)

        return lax.fori_loop(lo, hi, body, begin)

    def weight(lo, hi):
        shifted = [[], [], []]
        right = [[], [], []]
        for f in range(frames):
            line = [row_of(xf, f, r) for r in range(lo, hi + 2)]
            for r in range(lo, hi):
                v = bf[c, f, r + 1].astype(F32)
                shifted[0].append(from_right(v).astype(BF16))
                shifted[1].append(v.astype(BF16))
                shifted[2].append(from_left(v).astype(BF16))
                for i in range(3):
                    right[i].append(line[r - lo + i])
        left = jnp.concatenate([jnp.concatenate(x, axis=1) for x in shifted], axis=0)
        for i in range(3):
            rb[i * 3 * own : (i + 1) * 3 * own, :full] += lax.dot_general(
                left, jnp.concatenate(right[i], axis=1), (((1,), (1,)), ((), ())),
                preferred_element_type=F32,
            )

    sums = [(jnp.zeros((step, cells), F32),) * ntap] * (own // step)
    g_chan = []
    g_up = up_copies(1, bf.at[c, :, 1], bf.at[c, :, rows + 1])
    g_down = down_copies(1, bf.at[c, :, rows], bf.at[c, :, 0])
    base = 9 * own
    for t, (lo, hi) in enumerate(parts):
        with jax.named_scope("wait_c"):
            run(has_next, c_prev[t : t + 1], "wait_recv")
            run(has_prev, c_next[t : t + 1], "wait_recv")
        final = t == len(parts) - 1
        if final:
            run(has_prev, a_prev[1:2], "start")
            run(has_next, a_next[1:2], "start")
        with jax.named_scope("back"):
            sums = [back(q, lo, hi, sums[q]) for q in range(own // step)]
        lines = bf.at[c, :, 1 + lo : 1 + hi]
        sent = chan_copies(1 + t, lines, lines)
        g_chan += sent
        for copy in sent:
            copy.start()
        if t == 0:
            run(has_up, g_up, "start")
        if final:
            run(has_down, g_down, "start")
            whole = jnp.concatenate([sums[q][k] for k in range(ntap) for q in range(own // step)], axis=0)
            high = whole.astype(BF16)
            rest = whole - high.astype(F32)
            middle = rest.astype(BF16)
            low = (rest - middle.astype(F32)).astype(BF16)
            line = lax.dot_general(
                jnp.ones((16, 3 * cells), BF16), jnp.concatenate([high, middle, low], axis=1),
                (((1,), (1,)), ((), ())), preferred_element_type=F32,
            )
            for k in range(ntap):
                rb[base + k : base + k + 1, :own] = line[:1, k * own : (k + 1) * own]
        with jax.named_scope("wgt"):
            weight(lo, hi)

    def scatter(d):
        other, device = peer(d)
        src = rbb.at[pl.ds(pl.multiple_of(other * chunk, 16), chunk)]
        return remote(src, rv.at[d - 1], red_s.at[0, d - 1], red_r.at[0, d - 1], device)

    def gather(d):
        _, device = peer(d)
        dst = fin.at[pl.ds(pl.multiple_of(me * chunk, 16), chunk)]
        return remote(rs, dst, red_s.at[1, d - 1], red_r.at[1, d - 1], device)

    def each(make, what):
        def body(d, carry):
            getattr(make(d), what)()
            return carry

        lax.fori_loop(1, n, body, 0)

    spare, pieces, extra = plan
    packed = rb.shape[0] - extra
    if packed < rbb.shape[0]:
        rbb[packed:] = jnp.zeros((rbb.shape[0] - packed, rbb.shape[1]), BF16)
    if pieces:
        lanes = rb.shape[1]
        place = lax.broadcasted_iota(jnp.int32, (extra, lanes), 1)
        tail = rb[packed:]
        for t in range(pieces):
            mixed = jnp.where(
                place < full,
                rb[t * extra : (t + 1) * extra],
                pltpu.roll(tail, (full - t * spare) % lanes, 1),
            )
            rbb[t * extra : (t + 1) * extra] = mixed.astype(BF16)
    else:
        rbb[:packed] = rb[...].astype(BF16)
    for t in range(1, rounds):
        heard(t)
    each(scatter, "start")
    run(has_prev, a_prev[2:], "start")
    run(has_next, a_next[2:], "start")

    with jax.named_scope("wait_g"):
        for copy in g_chan:
            copy.wait_recv()
        run(has_down, g_up, "wait_recv")
        run(has_up, g_down, "wait_recv")

    def backward(f, carry):
        line = rows_of(bf, f)
        total = None
        for i in range(3):
            part = jnp.dot(wb[i], jnp.concatenate(line[2 - i : 2 - i + rows], axis=1),
                           preferred_element_type=F32)
            total = part if total is None else total + part
        for r in range(rows):
            seg = total[:, r * cells : (r + 1) * cells]
            h = from_right(seg[:own]) + seg[own : 2 * own] + from_left(seg[2 * own :])
            fg[f, r] = (ct[f + pad, r].astype(F32) + h).astype(BF16)
        return carry

    with jax.named_scope("bwd"):
        lax.fori_loop(0, frames, backward, 0, unroll=True)

    with jax.named_scope("wait_rs"):
        each(scatter, "wait_recv")

    here = pl.ds(pl.multiple_of(me * chunk, 16), chunk)
    total = lax.fori_loop(0, n - 1, lambda d, acc: acc + rv[d].astype(F32), rbb[here].astype(F32)) * scale
    rs[...] = total.astype(BF16)
    fin[here] = total.astype(BF16)
    each(gather, "start")

    with jax.named_scope("wait_a"):
        run(has_next, a_prev, "wait_recv")
        run(has_prev, a_next, "wait_recv")

    for q in range(own // step):
        part = pl.ds(q * step, step)

        def mix(r, carry, part=part):
            acts = [ac[g, r, part].astype(F32) for g in range(frames + 2 * pad)]
            for f in range(frames):
                total = None
                for k in range(ntap):
                    term = tb[k, part] * acts[f + k]
                    total = term if total is None else total + term
                mixed = total.astype(BF16).astype(F32)
                out[f, r, part] = (xf[c, f, r + 1, part].astype(F32) + mixed).astype(BF16)
            return carry

        lax.fori_loop(0, rows, mix, 0)

    with jax.named_scope("wait_ag"):
        each(gather, "wait_recv")
    if pieces:
        last = None
        for t in reversed(range(pieces)):
            v = fin[t * extra : (t + 1) * extra].astype(F32)
            rb[t * extra : (t + 1) * extra] = v
            v = pltpu.roll(v, (t * spare - full) % lanes, 1)
            last = v if last is None else jnp.where(place < (t + 1) * spare, v, last)
        rb[packed:] = last
    else:
        rb[...] = fin[:packed].astype(F32)
    for i in range(3):
        for j in range(3):
            top = (i * 3 + j) * own
            sg[i, j] = rb[top : top + own, :full]
    tg[...] = rb[base : base + ntap, :own]

    for copy in x_chan + g_chan:
        copy.wait_send()
    run(has_up, x_up + g_up, "wait_send")
    run(has_down, x_down + g_down, "wait_send")
    run(has_prev, c_prev + a_prev, "wait_send")
    run(has_next, c_next + a_next, "wait_send")
    each(scatter, "wait_send")
    each(gather, "wait_send")


def row_parts(rows):
    first = max(rows // 2, 1)
    second = first + max((rows - first) // 2, 0)
    cuts = sorted({0, first, second, rows})
    return list(zip(cuts[:-1], cuts[1:]))


def ship(*refs):
    sems = refs[8]
    copies = [pltpu.make_async_copy(refs[i], refs[i + 4], sems.at[i]) for i in range(4)]
    for copy in copies:
        copy.start()
    for copy in copies:
        copy.wait()


def on_device(field, cotangent, space_weight, time_weight):
    frames, rows, own, cells = field.shape
    nh, ns, nc = (lax.axis_size(a) for a in ("shard", "sub", "chan"))
    ntap = time_weight.shape[0]
    pad = ntap // 2
    full = own * nc
    n = nh * ns
    need = 9 * own + ntap
    lanes = -(-full // 128) * 128
    spare = lanes - full
    if spare and full % spare == 0:
        pieces = full // spare
        extra = -(-need // (16 * (pieces + 1))) * 16
        packed = extra * pieces
    else:
        pieces, extra, packed = 0, 0, -(-need // 16) * 16
    chunk = -(-packed // (16 * n)) * 16
    scale = float(frames * nh * rows * ns * cells) ** (-0.5)
    vmem = pl.BlockSpec(memory_space=pltpu.VMEM)
    dma = pltpu.SemaphoreType.DMA
    count = len(row_parts(rows))
    limit = 20 * 2**20 if rows * frames <= 16 else 56 * 2**20
    hbm = pl.BlockSpec(memory_space=pltpu.HBM)
    shapes = (
        (field.shape, BF16),
        (field.shape, BF16),
        ((3, 3, own, full), F32),
        ((ntap, own), F32),
    )
    held = pl.pallas_call(
        functools.partial(block, (nh, ns, nc, scale), (spare, pieces, extra)),
        out_shape=tuple(pltpu.VMEM(*x) for x in shapes),
        in_specs=[hbm] * 4,
        out_specs=(vmem,) * 4,
        scratch_shapes=[
            pltpu.VMEM((nc, frames, rows + 2, own, cells), BF16),
            pltpu.VMEM((nc, frames, rows + 2, own, cells), BF16),
            pltpu.VMEM((frames + 2 * pad, rows, own, cells), BF16),
            pltpu.VMEM((frames + 2 * pad, rows, own, cells), BF16),
            pltpu.VMEM((frames, rows, own, cells), F32),
            pltpu.VMEM((3, 3 * own, full), BF16),
            pltpu.VMEM((3, 3, full, full), BF16),
            pltpu.VMEM((3, 3 * own, full), BF16),
            pltpu.VMEM((ntap, own, cells), F32),
            pltpu.VMEM((packed + extra, lanes), F32),
            pltpu.VMEM((n * chunk, lanes), BF16),
            pltpu.VMEM((n - 1, chunk, lanes), BF16),
            pltpu.VMEM((chunk, lanes), BF16),
            pltpu.VMEM((n * chunk, lanes), BF16),
            pltpu.VMEM(space_weight.shape, BF16),
            pltpu.VMEM(time_weight.shape, BF16),
            pltpu.SemaphoreType.REGULAR((max(nh + ns - 3, 1),)),
            dma((4,)),
            dma((count + 1, nc - 1)),
            dma((count + 1, nc - 1)),
            dma((2, 2, nc)),
            dma((2, 2, nc)),
            dma((2 * count, 2)),
            dma((2 * count, 2)),
            dma((2, n - 1)),
            dma((2, n - 1)),
        ],
        compiler_params=pltpu.CompilerParams(
            collective_id=0, has_side_effects=True, vmem_limit_bytes=limit
        ),
    )(*(pltpu.with_memory_space_constraint(x, pltpu.HBM) for x in (field, cotangent, space_weight, time_weight)))
    return pl.pallas_call(
        ship,
        out_shape=tuple(jax.ShapeDtypeStruct(*x) for x in shapes),
        in_specs=[vmem] * 4,
        out_specs=(hbm,) * 4,
        scratch_shapes=[dma((4,))],
    )(*(pltpu.with_memory_space_constraint(x, pltpu.VMEM) for x in held))


def solution(mesh):
    placed = (
        P(("groups", "shard"), "sub", "chan", None),
        P(("groups", "shard"), "sub", "chan", None),
        P(),
        P(None, "chan"),
    )
    return jax.shard_map(
        on_device,
        mesh=mesh,
        in_specs=placed,
        out_specs=(
            P(("groups", "shard"), "sub", "chan", None),
            P(("groups", "shard"), "sub", "chan", None),
            P("groups", None, "chan", None),
            P("groups", "chan"),
        ),
        check_vma=False,
    )
```
